256 devices in a mesh: dp: 4 (over x), ep: 64 (over y, z, core).
Axes of the slice: x: 4, y: 4, z: 8, core: 2. Of those that a mesh axis runs over, the one named last changes fastest.
Arguments:
- queries: bfloat16 [8192, 36864], P('ep', 'dp'), may hold values from -40 to 40
- suffix_latent: bfloat16 [8192, 576], P('ep'), may hold values from -10 to 10
- page_pool: bfloat16 [512, 36864], P('ep'), may hold values from -6 to 6
- page_owner: int32 [64, 32], P('ep'), may hold values from 0 to 63, as said below
- page_slot: int32 [64, 32], P('ep'), may hold values from 0 to 7
- prefix_len: int32 [64], P('ep'), may hold values from 1025 to 2048, as said below
- moe_input: bfloat16 [4096, 3584], P(('dp', 'ep')), may hold values from -6 to 6
- expert_ids: int32 [4096, 8], P(('dp', 'ep')), may hold values from 0 to 63, all different within a row; in each aligned block of 16 rows (0 to 15, 16 to 31, ...) at most 2 rows name the same one
- gate_weights: float32 [4096, 8], P(('dp', 'ep')), may hold values from 0.1 to 0.6
- w_gate: bfloat16 [64, 3584, 1024], P('ep', None, 'dp'), may hold values from -0.09375 to 0.09375
- w_up: bfloat16 [64, 3584, 1024], P('ep', None, 'dp'), may hold values from -0.09375 to 0.09375
- w_down: bfloat16 [64, 1024, 3584], P('ep', 'dp'), may hold values from -0.1875 to 0.1875
Outputs:
- attn_context: bfloat16 [8192, 32768], P('ep', 'dp')
- moe_output: bfloat16 [4096, 3584], P(('dp', 'ep'))
The draws below stay inside these ranges and needn't reach their ends.
Inputs may be any that keep to these rules, and one draw needn't show every extreme that they name: `page_owner`: for a multiple m of the ep axis's size, the pages m, m + 1, ... of one request up to m + that size - 1 have distinct owners, so page k is the (k div that size)-th page of its request on its owner; entries past a request's prefix are valid page references too. `prefix_len`: some request has the longest prefix, 2048 tokens. `expert_ids`: in the 16 rows of one device no expert is named by more than 2 rows.
All inputs are finite; a program needn't handle non-finite values.
Results may differ from the reference program's by a relative error of at most 0.0057.
Values may be sent and summed in bfloat16 or wider, within the bound.
A program may use at most 128 MiB of HBM per device.

```python
import math
import jax
import jax.numpy as jnp
import numpy as np
from jax import lax

LATENT = 512
ROPE = 64
TOP = 8
HID = 3584
FFN = 1024
HEADS = 64
PAGE = 64
PMAX = 32
PAGES_DEV = 8
TQ = 128
TM = 16
EXPERTS = 64
CAP = 2
KD = 576
REQS = 64
TOK_A = 8192
TOK_M = 4096
N_EP = 64


def joint_attention(key):
    tokens = TQ * REQS
    key_width = LATENT + ROPE
    subkeys = jax.random.split(jax.random.fold_in(key, 7301), 2)
    suffix = jax.random.normal(subkeys[0], (tokens, key_width), jnp.float32)
    queries = jax.random.normal(subkeys[1], (tokens, HEADS, key_width), jnp.float32)
    return (queries.reshape(tokens, HEADS * key_width), suffix)


def draw_queries(key, part):
    return joint_attention(key)[0].astype(jnp.bfloat16)


def draw_suffix_latent(key, part):
    return joint_attention(key)[1].astype(jnp.bfloat16)


def draw_page_owner(key, part):
    request_keys = jax.random.split(jax.random.fold_in(key, 4409), REQS)
    permuted = jax.vmap(lambda single: jax.random.permutation(single, N_EP))(request_keys).astype(jnp.int32)
    column = jnp.arange(PMAX, dtype=jnp.int32) % N_EP
    return permuted[:, column]


def draw_prefix_len(key, part):
    subkeys = jax.random.split(jax.random.fold_in(key, 9127), 2)
    longest = PMAX * PAGE
    lengths = jax.random.randint(subkeys[0], (REQS,), longest // 2 + 1, longest + 1)
    picked = jax.random.randint(subkeys[1], (), 0, REQS)
    filled = jnp.arange(REQS, dtype=jnp.int32) == picked
    return jnp.where(filled, longest, lengths).astype(jnp.int32)


def with_ends(values, rng, smallest, high):
    dims = values.shape
    index_at = [jax.random.randint(jax.random.fold_in(rng, axis), (), 0, dims[axis]) for axis in range(len(dims))]
    values = values.at[tuple(index_at)].set(smallest)
    longest = dims.index(max(dims))
    index_at[longest] = (index_at[longest] + 1) % dims[longest]
    return values.at[tuple(index_at)].set(high)


def shard_levels(own_key, extent, cuts, smallest, largest):
    gain = 1.0
    for dim, shards_of in cuts:
        heights = jax.random.uniform(jax.random.fold_in(jax.random.fold_in(own_key, 6), dim), (shards_of,), jnp.float32, smallest / len(cuts), largest / len(cuts))
        gain = gain * jnp.repeat(jnp.exp(heights), extent[dim] // shards_of).reshape((-1,) + (1,) * (len(extent) - 1 - dim))
    return gain


def shared_out(key, own, number, rows, amount, top, limit, slope):
    sequence = jax.random.permutation(key, amount)
    packed, ordinary = load_shares(amount, rows * top, limit, slope, True), load_shares(amount, rows * top, limit, slope, False)
    places = jnp.arange(amount)

    def named(sizes, turn):
        used = int((sizes > 0).sum())
        fixed = max(1, used // 4)
        passed = fixed + (places - fixed + turn * (used - fixed)) % max(1, amount - fixed)
        return jnp.zeros((amount,), jnp.int32).at[sequence[jnp.where(places < fixed, places, passed)]].set(jnp.asarray(sizes, jnp.int32))

    sizes = jnp.where(number % 4 == 0, named(packed, number // 4), named(ordinary, number - number // 4 - 1))
    mixed = jax.random.permutation(jax.random.fold_in(own, 3), amount)
    giver, taker = mixed[0:amount // 2 * 2:2], mixed[1:amount // 2 * 2:2]
    slack = jnp.minimum(sizes[giver] - 1, limit - sizes[taker]) // 2
    slack = jnp.where((giver == sequence[0]) | (taker == sequence[0]) | (sizes[taker] == 0), 0, jnp.maximum(slack, 0))
    passed = jax.random.randint(jax.random.fold_in(own, 4), (amount // 2,), 0, 1 << 20) % (slack + 1)
    sizes = sizes.at[giver].add(-passed).at[taker].add(passed)
    items = jnp.searchsorted(jnp.cumsum(sizes), jnp.arange(rows * top), side="right").astype(jnp.int32)
    grid = items.reshape(top, rows).T
    grid = grid[jax.random.permutation(jax.random.fold_in(own, 1), rows)]
    turn = jax.random.randint(jax.random.fold_in(own, 2), (rows, 1), 0, top)
    return jnp.take_along_axis(grid, (jnp.arange(top)[None, :] + turn) % top, axis=1)


def load_shares(number_of, total, reach, skew, full):
    loads = [(1 << 20) // math.isqrt(standing ** skew) + 1 for standing in range(1, number_of + 1)]
    largest = reach if full else min(reach, max(-(-total // number_of), total * loads[0] // sum(loads)))
    least = 1 if total - largest >= number_of - 1 else 0
    given, spare = [largest] + [least] * (number_of - 1), total - largest - least * (number_of - 1)
    while spare > 0:
        free = [i for i in range(1, number_of) if given[i] < largest] or [i for i in range(1, number_of) if given[i] < reach]
        pool, remaining = sum([loads[i] for i in free]), spare
        for i in free:
            more = min(reach - given[i], max(1, remaining * loads[i] // pool), spare)
            given[i] = given[i] + more
            spare = spare - more
    return np.array(given)


def normal_values(rng, shape, scale, bound, shards=(), held_as=jnp.bfloat16):
    level = shard_levels(rng, shape, shards, -0.22, 0.18) if shards else 1.0
    drawn = jax.random.normal(rng, shape, jnp.float32) * scale * level
    return jnp.minimum(jnp.maximum(drawn, -bound), bound).astype(held_as)


def setup_inputs(seed: int = 0) -> dict:
    seeds = jax.random.split(jax.random.key(seed), 13)
    queries = draw_queries(jax.random.fold_in(seeds[12], 71), 0)
    suffix_latent = draw_suffix_latent(jax.random.fold_in(seeds[12], 71), 0)
    page_pool = normal_values(seeds[2], (REQS * PAGES_DEV, PAGE * KD), 1.0, 6.0, ((0, 64),))
    page_owner = draw_page_owner(jax.random.fold_in(seeds[12], 71), 0)
    page_slot = with_ends(jax.random.randint(seeds[4], (REQS, PMAX), 0, PAGES_DEV), jax.random.fold_in(seeds[4], 1), 0, PAGES_DEV - 1).astype(jnp.int32)
    prefix_len = draw_prefix_len(jax.random.fold_in(seeds[12], 71), 0)
    moe_input = normal_values(seeds[6], (TOK_M, HID), 1.0, 6.0, ((0, 256),))
    expert_ids_keys = jax.random.split(jax.random.fold_in(seeds[7], 1), TOK_M // TM)
    expert_ids_turns = jax.random.permutation(jax.random.fold_in(seeds[7], 3), TOK_M // TM)
    expert_ids = jax.vmap(lambda own, number: shared_out(jax.random.fold_in(seeds[7], 2), own, number, TM, EXPERTS, TOP, CAP, 2))(expert_ids_keys, expert_ids_turns).reshape((TOK_M, TOP))
    gate_weights = jnp.clip(0.1 + 0.5 * jax.random.uniform(seeds[8], (TOK_M, TOP), jnp.float32) ** shard_levels(seeds[8], (TOK_M, TOP), ((0, 256),), -0.2, 0.2), 0.1, 0.6)
    w_gate = normal_values(seeds[9], (EXPERTS, HID, FFN), HID ** -0.5, 0.09375, ((0, 64), (2, 4)))
    w_up = normal_values(seeds[10], (EXPERTS, HID, FFN), HID ** -0.5, 0.09375, ((0, 64), (2, 4)))
    w_down = normal_values(seeds[11], (EXPERTS, FFN, HID), FFN ** -0.5, 0.1875, ((0, 64), (1, 4)))
    return dict(queries=queries, suffix_latent=suffix_latent, page_pool=page_pool, page_owner=page_owner, page_slot=page_slot, prefix_len=prefix_len, moe_input=moe_input, expert_ids=expert_ids, gate_weights=gate_weights, w_gate=w_gate, w_up=w_up, w_down=w_down)


score_scale = 0.07216878364870322
neg_large = -1.0e30


def attend(query_rows, suffix_rows, prefix_keys, length):
    new_tokens = suffix_rows.shape[0]
    key_width = suffix_rows.shape[1]
    head_count = query_rows.shape[1] // key_width
    flat_queries = query_rows.reshape(new_tokens * head_count, key_width)
    all_keys = jnp.concatenate([prefix_keys, suffix_rows], axis=0)
    scores = lax.dot_general(flat_queries, all_keys, (((1,), (1,)), ((), ())), preferred_element_type=jnp.float32) * score_scale
    prefix_count = prefix_keys.shape[0]
    key_index = jnp.arange(prefix_count + new_tokens, dtype=jnp.int32)[None, :]
    row_token = (jnp.arange(new_tokens * head_count, dtype=jnp.int32) // head_count)[:, None]
    allowed = jnp.where(key_index < prefix_count, key_index < length, key_index - prefix_count <= row_token)
    masked = jnp.where(allowed, scores, neg_large)
    row_max = jnp.max(masked, axis=1, keepdims=True)
    exponent = jnp.where(allowed, jnp.exp(masked - row_max), 0.0)
    probs = (exponent / jnp.sum(exponent, axis=1, keepdims=True)).astype(jnp.bfloat16)
    context = jnp.dot(probs, all_keys[:, :LATENT], preferred_element_type=jnp.float32)
    return context.astype(jnp.bfloat16).reshape(new_tokens, head_count * LATENT)


def reference(queries, suffix_latent, page_pool, page_owner, page_slot, prefix_len, moe_input, expert_ids, gate_weights, w_gate, w_up, w_down):
    page_rows = page_pool.reshape(REQS * PAGES_DEV, PAGE, KD)
    query_blocks = queries.reshape(REQS, TQ, HEADS * KD)
    suffix_blocks = suffix_latent.reshape(REQS, TQ, KD)

    def one_request(inputs):
        query_rows, suffix_rows, owners, slot_ids, length = inputs
        rows_wanted = (owners * PAGES_DEV + slot_ids).astype(jnp.int32)
        prefix_keys = page_rows[rows_wanted].reshape(PMAX * PAGE, KD)
        return attend(query_rows, suffix_rows, prefix_keys, length)

    contexts = lax.map(one_request, (query_blocks, suffix_blocks, page_owner, page_slot, prefix_len))
    attn_context = contexts.reshape(TOK_A, HEADS * LATENT)

    block_count = TOK_M // TM
    routed = expert_ids.reshape(block_count, TM * TOP)
    onehot = (routed[:, :, None] == jnp.arange(EXPERTS, dtype=jnp.int32)[None, None, :]).astype(jnp.int32)
    slot_index = jnp.sum((jnp.cumsum(onehot, axis=1) - 1) * onehot, axis=2)
    position = (jnp.arange(block_count, dtype=jnp.int32)[:, None] * CAP + slot_index).reshape(-1).astype(jnp.int32)
    token_index = (jnp.arange(block_count * TM * TOP, dtype=jnp.int32) // TOP).astype(jnp.int32)
    flat_routed = routed.reshape(-1)
    row_table = jnp.full((EXPERTS, block_count * CAP), TOK_M, jnp.int32).at[flat_routed, position].set(token_index)
    weight_table = jnp.zeros((EXPERTS, block_count * CAP), jnp.float32).at[flat_routed, position].set(gate_weights.reshape(-1))
    padded = jnp.concatenate([moe_input, jnp.zeros((1, HID), moe_input.dtype)], axis=0)

    def one_expert(accumulated, inputs):
        rows_used, row_weight, gate_matrix, up_matrix, down_matrix = inputs
        chosen_rows = padded[rows_used]
        gate_proj = jnp.dot(chosen_rows, gate_matrix, preferred_element_type=jnp.float32)
        up_proj = jnp.dot(chosen_rows, up_matrix, preferred_element_type=jnp.float32)
        hidden = (jax.nn.silu(gate_proj) * up_proj).astype(jnp.bfloat16)
        expert_out = jnp.dot(hidden, down_matrix, preferred_element_type=jnp.float32).astype(jnp.bfloat16)
        accumulated = accumulated.at[rows_used].add(row_weight[:, None] * expert_out.astype(jnp.float32))
        return accumulated, None

    accumulated, unused = lax.scan(one_expert, jnp.zeros((TOK_M + 1, HID), jnp.float32), (row_table, weight_table, w_gate, w_up, w_down))
    moe_output = accumulated[:TOK_M].astype(jnp.bfloat16)
    return attn_context, moe_output
```

```python
import math

import jax
import jax.numpy as jnp
from jax import lax
from jax.experimental import pallas as pl
from jax.experimental.pallas import tpu as pltpu
from jax.sharding import PartitionSpec as P

LATENT = 512
KD = 576
PAGE = 64
SCALE = 0.07216878364870322
NEG = -1e30
LOG2E = 1.4426950408889634

NX = 4
NZ = 8
NG = 8
ROWS = 128
BLOCK = 16
REQ = 128
MESH = pl.DeviceIdType.MESH


def position():
    x = lax.axis_index("dp")
    ep = lax.axis_index("ep")
    core = lax.rem(ep, 2)
    z = lax.rem(lax.div(ep, 2), NZ)
    y = lax.div(ep, 2 * NZ)
    return x, y, z, core


def peers():
    x, y, z, core = position()
    g = y * 2 + core

    def along_z(d):
        other = lax.rem(z + d, NZ)
        return other, (x, (y * NZ + other) * 2 + core)

    def along_g(d):
        other = lax.rem(g + d, NG)
        return other, (x, (lax.div(other, 2) * NZ + z) * 2 + lax.rem(other, 2))

    def along_x(d):
        other = lax.rem(x + d, NX)
        return other, (other, (y * NZ + z) * 2 + core)

    return (x, z, g), (along_x, along_z, along_g)


def greet(along_x, along_z, along_g):
    barrier = pltpu.get_barrier_semaphore()

    def signal(dev):
        pl.semaphore_signal(barrier, inc=1, device_id=dev, device_id_type=MESH)

    def one(d, carry):
        signal(along_z(d)[1])
        signal(along_g(d)[1])
        return carry

    lax.fori_loop(1, 8, one, 0)
    signal(along_x(1)[1])
    signal(along_x(3)[1])
    return lambda: pl.semaphore_wait(barrier, 16)


def block_at(i):
    return pl.ds(pl.multiple_of(i * BLOCK, BLOCK), BLOCK)


def exchange(src, dst, cols, me, along, send_sem, recv_sem):
    def one(d, carry):
        other, dev = along(d)
        pltpu.make_async_remote_copy(
            src_ref=src.at[block_at(other), cols],
            dst_ref=dst.at[block_at(me), cols],
            send_sem=send_sem,
            recv_sem=recv_sem,
            device_id=dev,
            device_id_type=MESH,
        ).start()
        return carry

    lax.fori_loop(1, 8, one, 0)
    dst[block_at(me), cols] = src[block_at(me), cols]


def settle(ref, cols, sem):
    seven = ref.at[0 : 7 * BLOCK, cols]
    pltpu.make_async_copy(seven, seven, sem).wait()


def send(src, dst, send_sem, recv_sem, dev):
    copy = pltpu.make_async_remote_copy(
        src_ref=src, dst_ref=dst, send_sem=send_sem, recv_sem=recv_sem, device_id=dev, device_id_type=MESH
    )
    copy.start()
    return copy


def arrived(ref, sem):
    pltpu.make_async_copy(ref, ref, sem).wait()


def regroup():
    to = lax.broadcasted_iota(jnp.int32, (ROWS, ROWS), 0)
    of = lax.broadcasted_iota(jnp.int32, (ROWS, ROWS), 1)
    wanted = (lax.rem(to, 16) >> 1) * 16 + (to >> 4) * 2 + (to & 1)
    return jnp.where(of == wanted, 1.0, 0.0).astype(jnp.bfloat16)


def mm(a, b):
    return jnp.dot(a, b, preferred_element_type=jnp.float32)


def fetch_kernel(
    placed, tokens, req, sel, pool, wg_hbm, wu_hbm,
    hid_out, keys_out,
    rows, za, zb, xg, ps, pza, pzb, pya, kg, wg, wu,
    local, zs, zr, ys, yr, xs, xr, pzs, pzr, pys, pyr, pxs, pxr,
):
    (x, z, g), (along_x, along_z, along_g) = peers()
    greeted = greet(along_x, along_z, along_g)
    load_g = pltpu.make_async_copy(wg_hbm.at[0], wg, local.at[0])
    load_u = pltpu.make_async_copy(wu_hbm.at[0], wu, local.at[1])
    load_g.start()
    load_u.start()
    hid = tokens.shape[1]
    step = hid // 4
    chunks = [slice(0, REQ + step)] + [slice(REQ + step * i, REQ + step * (i + 1)) for i in range(1, 4)]
    own = [slice(REQ + step * i, REQ + step * (i + 1)) for i in range(4)]
    page_step = pool.shape[1] // 3
    page_chunks = [slice(page_step * i, page_step * (i + 1)) for i in range(3)]
    right, to_right = along_x(1)
    left, to_left = along_x(3)
    far = lax.rem(x + 2, NX)
    mine = xg.at[x]
    perm = regroup()
    copies = []

    rows[:, 0:REQ] = req[...]
    rows[:, REQ:] = mm(placed[...], tokens[...]).astype(jnp.bfloat16)
    greeted()
    for c in range(4):
        exchange(rows, za, chunks[c], z, along_z, zs.at[c], zr.at[c])

    def z_to_y(c):
        settle(za, chunks[c], zr.at[c])
        zb[:, chunks[c]] = mm(perm, za[:, chunks[c]]).astype(jnp.bfloat16)
        exchange(zb, mine, chunks[c], g, along_g, ys.at[c], yr.at[c])

    def y_to_x(c):
        settle(mine, chunks[c], yr.at[c])
        part = xg.at[x, :, own[c]]
        copies.append(send(part, part, xs.at[0, c], xr.at[0, c], to_right))
        copies.append(send(part, part, xs.at[1, c], xr.at[1, c], to_left))

    def forward(c):
        arrived(xg.at[left, :, own[c]], xr.at[0, c])
        part = xg.at[left, 0:64, own[c]]
        copies.append(send(part, part, xs.at[2, c], xr.at[2, c], to_right))
        arrived(xg.at[right, :, own[c]], xr.at[1, c])
        part = xg.at[right, 64:128, own[c]]
        copies.append(send(part, part, xs.at[3, c], xr.at[3, c], to_left))

    def ask():
        wanted = mm(perm, xg[x, :, 0:REQ]).astype(jnp.bfloat16)
        for c in range(3):
            ps[:, page_chunks[c]] = mm(wanted[:, 0:16], pool[:, page_chunks[c]]).astype(jnp.bfloat16)
            exchange(ps, pza, page_chunks[c], z, along_z, pzs.at[c], pzr.at[c])

    def page_z_to_y(c):
        settle(pza, page_chunks[c], pzr.at[c])
        pzb[:, page_chunks[c]] = mm(perm, pza[:, page_chunks[c]]).astype(jnp.bfloat16)
        exchange(pzb, pya, page_chunks[c], g, along_g, pys.at[c], pyr.at[c])

    def page_y_to_x(c):
        settle(pya, page_chunks[c], pyr.at[c])
        kg[x, :, page_chunks[c]] = mm(sel[...], pya[:, page_chunks[c]]).astype(jnp.bfloat16)
        part = kg.at[x, :, page_chunks[c]]
        copies.append(send(part, part, pxs.at[0, c], pxr.at[0, c], to_right))
        copies.append(send(part, part, pxs.at[1, c], pxr.at[1, c], to_left))

    def page_forward(c):
        arrived(kg.at[left, :, page_chunks[c]], pxr.at[0, c])
        part = kg.at[left, 0:32, page_chunks[c]]
        copies.append(send(part, part, pxs.at[2, c], pxr.at[2, c], to_right))
        arrived(kg.at[right, :, page_chunks[c]], pxr.at[1, c])
        part = kg.at[right, 32:64, page_chunks[c]]
        copies.append(send(part, part, pxs.at[3, c], pxr.at[3, c], to_left))

    def ffn(group):
        taken = xg[group, :, REQ:]
        gate = mm(taken, wg[...])
        up = mm(taken, wu[...])
        hid_out[group] = (gate / (1.0 + jnp.exp(-gate)) * up).astype(jnp.bfloat16)

    z_to_y(0)
    z_to_y(1)
    y_to_x(0)
    ask()
    z_to_y(2)
    y_to_x(1)
    forward(0)
    z_to_y(3)
    y_to_x(2)
    forward(1)
    y_to_x(3)
    load_g.wait()
    load_u.wait()
    ffn(x)
    page_z_to_y(0)
    forward(2)
    page_y_to_x(0)
    page_z_to_y(1)
    forward(3)
    page_y_to_x(1)
    page_forward(0)
    page_z_to_y(2)
    for c in range(4):
        arrived(xg.at[far, 0:64, own[c]], xr.at[2, c])
        arrived(xg.at[far, 64:128, own[c]], xr.at[3, c])
    page_y_to_x(2)

    def others(d, carry):
        ffn(lax.rem(x + d, NX))
        return carry

    lax.fori_loop(1, 4, others, 0)
    page_forward(1)
    page_forward(2)
    for c in range(3):
        arrived(kg.at[far, 0:32, page_chunks[c]], pxr.at[2, c])
        arrived(kg.at[far, 32:64, page_chunks[c]], pxr.at[3, c])
    store = pltpu.make_async_copy(kg, keys_out, local.at[2])
    store.start()
    for c in range(4):
        settle(rows, chunks[c], zs.at[c])
        settle(zb, chunks[c], ys.at[c])
    for c in range(3):
        settle(ps, page_chunks[c], pzs.at[c])
        settle(pzb, page_chunks[c], pys.at[c])
    for copy in copies:
        copy.wait_send()
    store.wait()


def finish_kernel(
    length, queries, suffix, kg, hidden, down, weights,
    context, out,
    qx, keys, causal, part_far, part_right, part_left, part_own, relay_left, relay_right, from_left, from_right,
    yb, yc, zb, zc,
    xs, xr, ys, yr, zs, zr,
):
    (x, z, g), (along_x, along_z, along_g) = peers()
    greeted = greet(along_x, along_z, along_g)
    tokens, hid = out.shape
    step = hid // 4
    cols = [slice(step * i, step * (i + 1)) for i in range(4)]
    right, to_right = along_x(1)
    left, to_left = along_x(3)
    far = lax.rem(x + 2, NX)
    perm = regroup()
    top, low = slice(0, 64), slice(64, 128)
    bf = jnp.bfloat16

    gates = weights[...]
    gate_1 = gates.astype(bf)
    rest = gates - gate_1.astype(jnp.float32)
    gate_2 = rest.astype(bf)
    gate_3 = (rest - gate_2.astype(jnp.float32)).astype(bf)

    def start_far(c):
        part_far[:, cols[c]] = mm(hidden[far], down[0, :, cols[c]]).astype(bf)
        send(part_far.at[top, cols[c]], relay_left.at[:, cols[c]], xs.at[0, c], xr.at[0, c], to_right)
        send(part_far.at[low, cols[c]], relay_right.at[:, cols[c]], xs.at[1, c], xr.at[1, c], to_left)

    def start_near(c):
        part_right[:, cols[c]] = mm(hidden[right], down[0, :, cols[c]]).astype(bf)
        part_left[:, cols[c]] = mm(hidden[left], down[0, :, cols[c]]).astype(bf)
        send(part_right.at[low, cols[c]], from_left.at[low, cols[c]], xs.at[2, c], xr.at[2, c], to_right)
        send(part_left.at[top, cols[c]], from_right.at[top, cols[c]], xs.at[3, c], xr.at[3, c], to_left)
        part_own[:, cols[c]] = mm(hidden[x], down[0, :, cols[c]])

    def relay(c):
        arrived(relay_left.at[:, cols[c]], xr.at[0, c])
        part_right[top, cols[c]] = (
            part_right[top, cols[c]].astype(jnp.float32) + relay_left[:, cols[c]].astype(jnp.float32)
        ).astype(bf)
        send(part_right.at[top, cols[c]], from_left.at[top, cols[c]], xs.at[4, c], xr.at[4, c], to_right)
        arrived(relay_right.at[:, cols[c]], xr.at[1, c])
        part_left[low, cols[c]] = (
            part_left[low, cols[c]].astype(jnp.float32) + relay_right[:, cols[c]].astype(jnp.float32)
        ).astype(bf)
        send(part_left.at[low, cols[c]], from_right.at[low, cols[c]], xs.at[5, c], xr.at[5, c], to_left)

    def to_y(c):
        arrived(from_left.at[low, cols[c]], xr.at[2, c])
        arrived(from_right.at[top, cols[c]], xr.at[3, c])
        arrived(from_left.at[top, cols[c]], xr.at[4, c])
        arrived(from_right.at[low, cols[c]], xr.at[5, c])
        yb[:, cols[c]] = (
            part_own[:, cols[c]]
            + from_left[:, cols[c]].astype(jnp.float32)
            + from_right[:, cols[c]].astype(jnp.float32)
        ).astype(bf)
        exchange(yb, yc, cols[c], g, along_g, ys.at[c], yr.at[c])

    def to_z(c):
        settle(yc, cols[c], yr.at[c])
        zb[:, cols[c]] = mm(perm, yc[:, cols[c]]).astype(bf)
        exchange(zb, zc, cols[c], z, along_z, zs.at[c], zr.at[c])

    def combine(c):
        settle(zc, cols[c], zr.at[c])
        back = zc[:, cols[c]]
        out[:, cols[c]] = (mm(gate_1, back) + mm(gate_2, back) + mm(gate_3, back)).astype(bf)

    lanes = lax.broadcasted_iota(jnp.int32, (64, 64), 1)
    line = lax.broadcasted_iota(jnp.int32, (64, 64), 0)

    def gather_keys():
        for q in range(4):
            for j in range(8):
                at = slice((q * 8 + j) * 64, (q * 8 + j + 1) * 64)
                keys[at, 0:KD] = kg[q, :, j * KD : (j + 1) * KD]
                place = (line >> 1) * PAGE + q * 16 + (line & 1) * 8 + j
                keys[at, KD : KD + 64] = jnp.where((lanes == 0) & (place >= length[0]), NEG, 0.0).astype(bf)
        keys[2048:2176, 0:KD] = suffix[...]
        keys[2048:2176, KD : KD + 64] = jnp.zeros((128, 64), bf)
        token = lax.broadcasted_iota(jnp.int32, (256, 128), 0) & 127
        later = lax.broadcasted_iota(jnp.int32, (256, 128), 1) > token
        causal[...] = jnp.where(later, NEG, 0.0)
        one = jnp.where(lax.broadcasted_iota(jnp.int32, (128, 64), 1) == 0, 1.0, 0.0).astype(bf)
        for h in range(16):
            qx[h * 128 : (h + 1) * 128, 0:KD] = queries[:, h * KD : (h + 1) * KD]
            qx[h * 128 : (h + 1) * 128, KD : KD + 64] = one

    def attend(i):
        q = qx[pl.ds(pl.multiple_of(i * 256, 256), 256), :]
        last = (((1,), (1,)), ((), ()))
        near = lax.dot_general(q, keys[2048:2176, :], last, preferred_element_type=jnp.float32) + causal[...]
        past = lax.dot_general(q, keys[0:2048, :], last, preferred_element_type=jnp.float32)
        peak = jnp.maximum(jnp.max(past, axis=1, keepdims=True), jnp.max(near, axis=1, keepdims=True))
        shift = peak * (SCALE * LOG2E)
        past = jnp.exp2(past * (SCALE * LOG2E) - shift)
        near = jnp.exp2(near * (SCALE * LOG2E) - shift)
        total = jnp.sum(past, axis=1, keepdims=True) + jnp.sum(near, axis=1, keepdims=True)
        got = mm(past.astype(bf), keys[0:2048, 0:LATENT]) + mm(near.astype(bf), keys[2048:2176, 0:LATENT])
        got = (got / total).astype(bf)
        at = pl.multiple_of(i * 1024, 1024)
        context[:, pl.ds(at, 512)] = got[0:128]
        context[:, pl.ds(at + 512, 512)] = got[128:256]

    def first():
        relay(0)
        start_near(1)
        start_far(2)

    def second():
        to_y(0)
        relay(1)
        start_near(2)
        start_far(3)

    def third():
        to_z(0)
        to_y(1)
        relay(2)
        start_near(3)

    def fourth():
        to_z(1)
        to_y(2)
        relay(3)

    greeted()
    start_far(0)
    start_near(0)
    start_far(1)
    gather_keys()

    @pl.loop(0, 4)
    def _(i):
        attend(2 * i)
        attend(2 * i + 1)
        for at, act in enumerate((first, second, third, fourth)):
            pl.when(i == at)(act)

    combine(0)
    to_z(2)
    to_y(3)
    combine(1)
    to_z(3)
    combine(2)
    combine(3)
    for c in range(4):
        settle(yb, cols[c], ys.at[c])
        settle(zb, cols[c], zs.at[c])
        arrived(part_far.at[top, cols[c]], xs.at[0, c])
        arrived(part_far.at[low, cols[c]], xs.at[1, c])
        arrived(part_right.at[low, cols[c]], xs.at[2, c])
        arrived(part_left.at[top, cols[c]], xs.at[3, c])
        arrived(part_right.at[top, cols[c]], xs.at[4, c])
        arrived(part_left.at[low, cols[c]], xs.at[5, c])


def device_of_row(row, z_first):
    outer, inner = row // 16, (row % 16) // 2
    z, g = (outer, inner) if z_first else (inner, outer)
    return ((g // 2) * NZ + z) * 2 + g % 2


def routing(expert_ids, gate_weights):
    tok_count = expert_ids.shape[0]
    row = jnp.arange(ROWS, dtype=jnp.int32)
    hit = expert_ids[:, :, None] == device_of_row(row, True)[None, None, :]
    named = jnp.any(hit, axis=1)
    earlier = jnp.arange(tok_count)[:, None] > jnp.arange(tok_count)[None, :]
    before = jnp.sum((earlier[:, :, None] & named[None, :, :]).astype(jnp.int32), axis=1)
    placed = named & (before == row[None, :] % 2)
    weight = jnp.sum(jnp.where(hit & placed[:, None, :], gate_weights[:, :, None], 0.0), axis=1)
    return placed.astype(jnp.bfloat16).T, weight


def requests(page_owner, page_slot):
    owner, slot = page_owner[0], page_slot[0]
    row = jnp.arange(ROWS, dtype=jnp.int32)
    asked = jnp.sum(
        jnp.where(owner[None, :] == device_of_row(row, True)[:, None], slot[None, :] + 1, 0), axis=1
    )
    lane = jnp.arange(REQ, dtype=jnp.int32)
    req = (asked[:, None] == lane[None, :] // 2 + 1) & (row[:, None] % 2 == lane[None, :] % 2)
    half = jnp.arange(2 * owner.shape[0], dtype=jnp.int32)
    sel = (jnp.repeat(owner, 2)[:, None] == device_of_row(row, False)[None, :]) & (
        half[:, None] % 2 == row[None, :] % 2
    )
    return (req & (lane < 16)[None, :]).astype(jnp.bfloat16), sel.astype(jnp.bfloat16)


def on_device(
    queries,
    suffix_latent,
    page_pool,
    page_owner,
    page_slot,
    prefix_len,
    moe_input,
    expert_ids,
    gate_weights,
    w_gate,
    w_up,
    w_down,
):
    bf, f32 = jnp.bfloat16, jnp.float32
    hid, unit = w_gate.shape[1:]
    placed, weight = routing(expert_ids, gate_weights)
    req, sel = requests(page_owner, page_slot)
    quarter = page_pool.shape[1] // NX
    pool = lax.dynamic_slice_in_dim(page_pool, lax.axis_index("dp") * quarter, quarter, axis=1)
    pool = pool.reshape(2 * page_pool.shape[0], quarter // 2)
    wide = pool.shape[1]
    vmem = pl.BlockSpec(memory_space=pltpu.VMEM)
    anyspace = pl.BlockSpec(memory_space=pl.ANY)
    dma = pltpu.SemaphoreType.DMA
    hidden, kg = pl.pallas_call(
        fetch_kernel,
        out_shape=(
            jax.ShapeDtypeStruct((NX, ROWS, unit), bf),
            jax.ShapeDtypeStruct((NX, 64, wide), bf),
        ),
        in_specs=[vmem] * 5 + [anyspace] * 2,
        out_specs=(vmem, anyspace),
        scratch_shapes=[
            pltpu.VMEM((ROWS, REQ + hid), bf),
            pltpu.VMEM((ROWS, REQ + hid), bf),
            pltpu.VMEM((ROWS, REQ + hid), bf),
            pltpu.VMEM((NX, ROWS, REQ + hid), bf),
            pltpu.VMEM((ROWS, wide), bf),
            pltpu.VMEM((ROWS, wide), bf),
            pltpu.VMEM((ROWS, wide), bf),
            pltpu.VMEM((ROWS, wide), bf),
            pltpu.VMEM((NX, 64, wide), bf),
            pltpu.VMEM((hid, unit), bf),
            pltpu.VMEM((hid, unit), bf),
            dma((3,)),
            dma((4,)), dma((4,)), dma((4,)), dma((4,)), dma((4, 4)), dma((4, 4)),
            dma((3,)), dma((3,)), dma((3,)), dma((3,)), dma((4, 3)), dma((4, 3)),
        ],
        compiler_params=pltpu.CompilerParams(
            collective_id=0, has_side_effects=True, vmem_limit_bytes=48 * 2**20
        ),
        name="fetch",
    )(placed, moe_input, req, sel, pool, w_gate, w_up)
    return pl.pallas_call(
        finish_kernel,
        out_shape=(
            jax.ShapeDtypeStruct((queries.shape[0], queries.shape[1] // KD * LATENT), bf),
            jax.ShapeDtypeStruct(moe_input.shape, bf),
        ),
        in_specs=[pl.BlockSpec(memory_space=pltpu.SMEM)] + [vmem] * 6,
        out_specs=(vmem, vmem),
        scratch_shapes=[
            pltpu.VMEM((2048, 640), bf),
            pltpu.VMEM((2176, 640), bf),
            pltpu.VMEM((256, 128), f32),
            pltpu.VMEM((ROWS, hid), bf),
            pltpu.VMEM((ROWS, hid), bf),
            pltpu.VMEM((ROWS, hid), bf),
            pltpu.VMEM((ROWS, hid), f32),
            pltpu.VMEM((64, hid), bf),
            pltpu.VMEM((64, hid), bf),
            pltpu.VMEM((ROWS, hid), bf),
            pltpu.VMEM((ROWS, hid), bf),
            pltpu.VMEM((ROWS, hid), bf),
            pltpu.VMEM((ROWS, hid), bf),
            pltpu.VMEM((ROWS, hid), bf),
            pltpu.VMEM((ROWS, hid), bf),
            dma((6, 4)), dma((6, 4)), dma((4,)), dma((4,)), dma((4,)), dma((4,)),
        ],
        compiler_params=pltpu.CompilerParams(
            collective_id=1, has_side_effects=True, vmem_limit_bytes=56 * 2**20
        ),
        name="finish",
    )(prefix_len, queries, suffix_latent, kg, hidden, w_down, weight)


def solution(mesh):
    return jax.shard_map(
        on_device,
        mesh=mesh,
        in_specs=(
            P("ep", "dp"),
            P("ep", None),
            P("ep", None),
            P("ep", None),
            P("ep", None),
            P("ep"),
            P(("dp", "ep"), None),
            P(("dp", "ep"), None),
            P(("dp", "ep"), None),
            P("ep", None, "dp"),
            P("ep", None, "dp"),
            P("ep", "dp", None),
        ),
        out_specs=(P("ep", "dp"), P(("dp", "ep"), None)),
        check_vma=False,
    )
```

```python
import math

import jax
import jax.numpy as jnp
from jax import lax
from jax.experimental import pallas as pl
from jax.experimental.pallas import tpu as pltpu
from jax.sharding import PartitionSpec as P

LATENT = 512
KD = 576
PAGE = 64
SCALE = 0.07216878364870322
NEG = -1e30
LOG2E = 1.4426950408889634

NX = 4
NZ = 8
NG = 8
ROWS = 128
BLOCK = 16
REQ = 128
DISPATCH = (512, 512, 512, 1024, 1024)
PAGE_PARTS = 3
COMBINE = (1024, 1024, 512, 512, 512)
MESH = pl.DeviceIdType.MESH


def position():
    x = lax.axis_index("dp")
    ep = lax.axis_index("ep")
    core = lax.rem(ep, 2)
    z = lax.rem(lax.div(ep, 2), NZ)
    y = lax.div(ep, 2 * NZ)
    return x, y, z, core


def peers():
    x, y, z, core = position()
    g = y * 2 + core

    def along_z(d):
        other = lax.rem(z + d, NZ)
        return other, (x, (y * NZ + other) * 2 + core)

    def along_g(d):
        other = lax.rem(g + d, NG)
        return other, (x, (lax.div(other, 2) * NZ + z) * 2 + lax.rem(other, 2))

    def along_x(d):
        other = lax.rem(x + d, NX)
        return other, (other, (y * NZ + z) * 2 + core)

    return (x, z, g), (along_x, along_z, along_g)


def greet(along_x, along_z, along_g):
    barrier = pltpu.get_barrier_semaphore()

    def signal(dev):
        pl.semaphore_signal(barrier, inc=1, device_id=dev, device_id_type=MESH)

    def one(d, carry):
        signal(along_z(d)[1])
        signal(along_g(d)[1])
        return carry

    lax.fori_loop(1, 8, one, 0)
    signal(along_x(1)[1])
    signal(along_x(3)[1])
    return lambda: pl.semaphore_wait(barrier, 16)


def block_at(i):
    return pl.ds(pl.multiple_of(i * BLOCK, BLOCK), BLOCK)


def exchange(src, dst, cols, me, along, send_sem, recv_sem):
    def one(d, carry):
        other, dev = along(d)
        pltpu.make_async_remote_copy(
            src_ref=src.at[block_at(other), cols],
            dst_ref=dst.at[block_at(me), cols],
            send_sem=send_sem,
            recv_sem=recv_sem,
            device_id=dev,
            device_id_type=MESH,
        ).start()
        return carry

    lax.fori_loop(1, 8, one, 0)
    dst[block_at(me), cols] = src[block_at(me), cols]


def settle(ref, cols, sem):
    seven = ref.at[0 : 7 * BLOCK, cols]
    pltpu.make_async_copy(seven, seven, sem).wait()


def send(src, dst, send_sem, recv_sem, dev):
    copy = pltpu.make_async_remote_copy(
        src_ref=src, dst_ref=dst, send_sem=send_sem, recv_sem=recv_sem, device_id=dev, device_id_type=MESH
    )
    copy.start()
    return copy


def arrived(ref, sem):
    pltpu.make_async_copy(ref, ref, sem).wait()


def regroup():
    to = lax.broadcasted_iota(jnp.int32, (ROWS, ROWS), 0)
    of = lax.broadcasted_iota(jnp.int32, (ROWS, ROWS), 1)
    wanted = (lax.rem(to, 16) >> 1) * 16 + (to >> 4) * 2 + (to & 1)
    return jnp.where(of == wanted, 1.0, 0.0).astype(jnp.bfloat16)


def mm(a, b):
    return jnp.dot(a, b, preferred_element_type=jnp.float32)


def nt(a, b):
    return lax.dot_general(a, b, (((1,), (1,)), ((), ())), preferred_element_type=jnp.float32)


def iota(shape, dim):
    return lax.broadcasted_iota(jnp.int32, shape, dim)


def device_of(outer, inner, z_first):
    z, g = (outer, inner) if z_first else (inner, outer)
    return ((g >> 1) * NZ + z) * 2 + (g & 1)


def row_device(shape, dim, z_first):
    row = iota(shape, dim)
    return device_of(row >> 4, (row >> 1) & 7, z_first)


def identity(size):
    return jnp.where(iota((size, size), 0) == iota((size, size), 1), 1.0, 0.0).astype(jnp.bfloat16)


def spans(sizes, start=0):
    found = []
    for size in sizes:
        found.append(slice(start, start + size))
        start += size
    return found


def whole_kernel(
    length, ids, gates, owner, slot, tokens, pool_hbm, wg_hbm, wu_hbm, wd_hbm, q_hbm, suffix,
    context, out,
    rows, za, zb, xg, pool, ps, pza, pzb, pya, kg, wg, wu, wd, hidden,
    queries, qx, keys, causal,
    part_far, part_right, part_left, near_right, near_left, part_own, relay_left, relay_right, from_left, from_right,
    cy, cya, cz, cza,
    local, zs, zr, ys, yr, xs, xr, pzs, pzr, pys, pyr, pxs, pxr, rs, rr, cys, cyr, czs, czr,
):
    (x, z, g), (along_x, along_z, along_g) = peers()
    greeted = greet(along_x, along_z, along_g)
    bf, f32 = jnp.bfloat16, jnp.float32
    half_page = pool.shape[2]
    loads = [
        pltpu.make_async_copy(
            pool_hbm.at[:, pl.ds(pl.multiple_of(x * (2 * half_page) + i * half_page, 128), half_page)],
            pool.at[i],
            local.at[i],
        )
        for i in range(2)
    ]
    loads += [
        pltpu.make_async_copy(wg_hbm.at[0], wg, local.at[2]),
        pltpu.make_async_copy(wu_hbm.at[0], wu, local.at[3]),
        pltpu.make_async_copy(wd_hbm.at[0], wd, local.at[4]),
        pltpu.make_async_copy(q_hbm, queries, local.at[5]),
    ]
    for load in loads:
        load.start()
    tok_count, hid = tokens.shape
    out_chunks = spans([REQ + DISPATCH[0], *DISPATCH[1:]])
    own = spans(DISPATCH, REQ)
    page_chunks = spans([half_page // PAGE_PARTS] * PAGE_PARTS)
    cols = spans(COMBINE)
    right, to_right = along_x(1)
    left, to_left = along_x(3)
    far = lax.rem(x + 2, NX)
    mine = xg.at[x]
    perm = regroup()
    top, low = slice(0, 64), slice(64, 128)

    expert = row_device((ROWS, tok_count), 0, True)
    hits = [ids[k : k + 1, :] == expert for k in range(ids.shape[0])]
    named = hits[0]
    for hit in hits[1:]:
        named = named | hit
    below = (iota((tok_count, tok_count), 0) < iota((tok_count, tok_count), 1)).astype(f32).astype(bf)
    before = mm(named.astype(f32).astype(bf), below)
    placed = named & (before == (iota((ROWS, tok_count), 0) & 1).astype(f32))
    page_count = owner.shape[1]
    asks = owner[...] == row_device((ROWS, page_count), 0, True)
    asked = jnp.sum(jnp.where(asks, slot[...] + 1, 0), axis=1, keepdims=True)
    lane = iota((ROWS, REQ), 1)
    row = iota((ROWS, REQ), 0)
    req = (lane < 16) & ((lane & 7) + 1 == asked) & ((lane >> 3) == (row & 1))
    rows[:, 0:REQ] = req.astype(f32).astype(bf)
    rows[:, REQ:] = mm(placed.astype(f32).astype(bf), tokens[...]).astype(bf)
    greeted()
    for c in range(len(out_chunks)):
        exchange(rows, za, out_chunks[c], z, along_z, zs.at[c], zr.at[c])

    weight = jnp.zeros((ROWS, tok_count), f32)
    for k, hit in enumerate(hits):
        weight = weight + jnp.where(hit & placed, gates[k : k + 1, :], 0.0)
    gate_1 = weight.astype(bf)
    rest = weight - gate_1.astype(f32)
    gate_2 = rest.astype(bf)
    gate_3 = (rest - gate_2.astype(f32)).astype(bf)
    eye = identity(tok_count)
    gate_1, gate_2, gate_3 = (nt(eye, part).astype(bf) for part in (gate_1, gate_2, gate_3))
    holds = (owner[...] == row_device((ROWS, page_count), 0, False)).astype(f32).astype(bf)
    spread = ((iota((64, page_count), 0) >> 1) == iota((64, page_count), 1)).astype(f32).astype(bf)
    sel = jnp.where((iota((64, ROWS), 0) & 1) == (iota((64, ROWS), 1) & 1), nt(spread, holds), 0.0).astype(bf)

    def z_to_y(c):
        settle(za, out_chunks[c], zr.at[c])
        zb[:, out_chunks[c]] = mm(perm, za[:, out_chunks[c]]).astype(bf)
        exchange(zb, mine, out_chunks[c], g, along_g, ys.at[c], yr.at[c])

    def y_to_x(c):
        settle(mine, out_chunks[c], yr.at[c])
        part = xg.at[x, :, own[c]]
        send(part, part, xs.at[0, c], xr.at[0, c], to_right)
        send(part, part, xs.at[1, c], xr.at[1, c], to_left)

    def forward(c):
        arrived(xg.at[left, :, own[c]], xr.at[0, c])
        part = xg.at[left, top, own[c]]
        send(part, part, xs.at[2, c], xr.at[2, c], to_right)
        arrived(xg.at[right, :, own[c]], xr.at[1, c])
        part = xg.at[right, low, own[c]]
        send(part, part, xs.at[3, c], xr.at[3, c], to_left)

    def ask():
        wanted = mm(perm, xg[x, :, 0:REQ]).astype(bf)
        loads[0].wait()
        loads[1].wait()
        for c in range(PAGE_PARTS):
            ps[:, page_chunks[c]] = (
                mm(wanted[:, 0:8], pool[0, :, page_chunks[c]]) + mm(wanted[:, 8:16], pool[1, :, page_chunks[c]])
            ).astype(bf)
            exchange(ps, pza, page_chunks[c], z, along_z, pzs.at[c], pzr.at[c])

    def page_z_to_y(c):
        settle(pza, page_chunks[c], pzr.at[c])
        pzb[:, page_chunks[c]] = mm(perm, pza[:, page_chunks[c]]).astype(bf)
        exchange(pzb, pya, page_chunks[c], g, along_g, pys.at[c], pyr.at[c])

    def page_y_to_x(c):
        settle(pya, page_chunks[c], pyr.at[c])
        kg[x, :, page_chunks[c]] = mm(sel, pya[:, page_chunks[c]]).astype(bf)
        part = kg.at[x, :, page_chunks[c]]
        send(part, part, pxs.at[0, c], pxr.at[0, c], to_right)
        send(part, part, pxs.at[1, c], pxr.at[1, c], to_left)

    def page_forward(c):
        arrived(kg.at[left, :, page_chunks[c]], pxr.at[0, c])
        part = kg.at[left, 0:32, page_chunks[c]]
        send(part, part, pxs.at[2, c], pxr.at[2, c], to_right)
        arrived(kg.at[right, :, page_chunks[c]], pxr.at[1, c])
        part = kg.at[right, 32:64, page_chunks[c]]
        send(part, part, pxs.at[3, c], pxr.at[3, c], to_left)

    def ffn(group):
        taken = xg[group, :, REQ:]
        gate = mm(taken, wg[...])
        up = mm(taken, wu[...])
        hidden[group] = (gate / (1.0 + jnp.exp(-gate)) * up).astype(bf)

    def start_far(c):
        part_far[:, cols[c]] = mm(hidden[far], wd[:, cols[c]]).astype(bf)
        send(part_far.at[top, cols[c]], relay_left.at[:, cols[c]], rs.at[0, c], rr.at[0, c], to_right)
        send(part_far.at[low, cols[c]], relay_right.at[:, cols[c]], rs.at[1, c], rr.at[1, c], to_left)

    def start_near(c):
        part_right[:, cols[c]] = mm(hidden[right], wd[:, cols[c]])
        part_left[:, cols[c]] = mm(hidden[left], wd[:, cols[c]])
        near_right[low, cols[c]] = part_right[low, cols[c]].astype(bf)
        near_left[top, cols[c]] = part_left[top, cols[c]].astype(bf)
        send(near_right.at[low, cols[c]], from_left.at[low, cols[c]], rs.at[2, c], rr.at[2, c], to_right)
        send(near_left.at[top, cols[c]], from_right.at[top, cols[c]], rs.at[3, c], rr.at[3, c], to_left)
        part_own[:, cols[c]] = mm(hidden[x], wd[:, cols[c]])

    def relay(c):
        arrived(relay_left.at[:, cols[c]], rr.at[0, c])
        near_right[top, cols[c]] = (part_right[top, cols[c]] + relay_left[:, cols[c]].astype(f32)).astype(bf)
        send(near_right.at[top, cols[c]], from_left.at[top, cols[c]], rs.at[4, c], rr.at[4, c], to_right)
        arrived(relay_right.at[:, cols[c]], rr.at[1, c])
        near_left[low, cols[c]] = (part_left[low, cols[c]] + relay_right[:, cols[c]].astype(f32)).astype(bf)
        send(near_left.at[low, cols[c]], from_right.at[low, cols[c]], rs.at[5, c], rr.at[5, c], to_left)

    def to_y(c):
        arrived(from_left.at[low, cols[c]], rr.at[2, c])
        arrived(from_right.at[top, cols[c]], rr.at[3, c])
        arrived(from_left.at[top, cols[c]], rr.at[4, c])
        arrived(from_right.at[low, cols[c]], rr.at[5, c])
        cy[:, cols[c]] = (
            part_own[:, cols[c]] + from_left[:, cols[c]].astype(f32) + from_right[:, cols[c]].astype(f32)
        ).astype(bf)
        exchange(cy, cya, cols[c], g, along_g, cys.at[c], cyr.at[c])

    def to_z(c):
        settle(cya, cols[c], cyr.at[c])
        cz[:, cols[c]] = mm(perm, cya[:, cols[c]]).astype(bf)
        exchange(cz, cza, cols[c], z, along_z, czs.at[c], czr.at[c])

    def combine(c):
        settle(cza, cols[c], czr.at[c])
        back = cza[:, cols[c]]
        out[:, cols[c]] = (mm(gate_1, back) + mm(gate_2, back) + mm(gate_3, back)).astype(bf)

    def place_queries():
        loads[5].wait()
        one = jnp.where(iota((128, 64), 1) == 0, 1.0, 0.0).astype(bf)
        for h in range(16):
            qx[h * 128 : (h + 1) * 128, 0:KD] = queries[:, h * KD : (h + 1) * KD]
            qx[h * 128 : (h + 1) * 128, KD : KD + 64] = one
        causal[...] = jnp.where(iota((256, 128), 1) > (iota((256, 128), 0) & 127), NEG, 0.0)
        keys[2048:2176, 0:KD] = nt(identity(128), suffix[...]).astype(bf)
        keys[2048:2176, KD : KD + 64] = jnp.zeros((128, 64), bf)

    def gather_keys():
        lanes, line = iota((64, 64), 1), iota((64, 64), 0)
        for q in range(4):
            for j in range(8):
                at = slice((q * 8 + j) * 64, (q * 8 + j + 1) * 64)
                keys[at, 0:KD] = kg[q, :, j * KD : (j + 1) * KD]
                place = (line >> 1) * PAGE + q * 16 + (line & 1) * 8 + j
                keys[at, KD : KD + 64] = jnp.where((lanes == 0) & (place >= length[0]), NEG, 0.0).astype(bf)

    def attend(i):
        q = qx[pl.ds(pl.multiple_of(i * 256, 256), 256), :]
        near = nt(q, keys[2048:2176, :]) + causal[...]
        past = nt(q, keys[0:2048, :])
        peak = jnp.maximum(jnp.max(past, axis=1, keepdims=True), jnp.max(near, axis=1, keepdims=True))
        shift = peak * (SCALE * LOG2E)
        past = jnp.exp2(past * (SCALE * LOG2E) - shift)
        near = jnp.exp2(near * (SCALE * LOG2E) - shift)
        total = jnp.sum(past, axis=1, keepdims=True) + jnp.sum(near, axis=1, keepdims=True)
        got = mm(past.astype(bf), keys[0:2048, 0:LATENT]) + mm(near.astype(bf), keys[2048:2176, 0:LATENT])
        got = (got / total).astype(bf)
        at = pl.multiple_of(i * 1024, 1024)
        context[:, pl.ds(at, 512)] = got[0:128]
        context[:, pl.ds(at + 512, 512)] = got[128:256]

    def wait_far():
        for c in range(len(own)):
            arrived(xg.at[far, top, own[c]], xr.at[2, c])
            arrived(xg.at[far, low, own[c]], xr.at[3, c])

    def wait_keys():
        for c in range(PAGE_PARTS):
            arrived(kg.at[far, 0:32, page_chunks[c]], pxr.at[2, c])
            arrived(kg.at[far, 32:64, page_chunks[c]], pxr.at[3, c])

    def wait_weights():
        for i in (2, 3, 4):
            loads[i].wait()

    z_to_y(0)
    y_to_x(0)
    z_to_y(1)
    y_to_x(1)
    z_to_y(2)
    place_queries()
    forward(0)
    y_to_x(2)
    z_to_y(3)
    forward(1)
    ask()
    y_to_x(3)
    z_to_y(4)
    y_to_x(4)
    forward(2)
    page_z_to_y(0)
    forward(3)
    page_y_to_x(0)
    page_z_to_y(1)
    forward(4)
    page_forward(0)
    wait_weights()
    ffn(right)
    wait_far()
    page_y_to_x(1)
    page_z_to_y(2)
    ffn(left)
    ffn(x)
    ffn(far)
    start_far(0)
    page_y_to_x(2)
    page_forward(1)
    page_forward(2)
    start_near(0)
    relay(0)
    start_far(1)
    start_near(1)
    wait_keys()
    gather_keys()

    def beside_2():
        to_y(0)
        relay(1)
        start_far(2)

    def beside_3():
        start_far(3)
        start_near(2)
        to_z(0)
        start_far(4)
        to_y(1)

    def beside_4():
        relay(2)
        start_near(3)
        relay(3)
        to_z(1)
        start_near(4)
        relay(4)
        to_y(2)

    def beside_5():
        combine(0)
        to_z(2)
        to_y(3)
        to_y(4)
        to_z(3)
        combine(1)
        to_z(4)

    def beside_6():
        combine(2)
        combine(3)

    @pl.loop(0, 8)
    def _(i):
        attend(i)
        pl.when(i == 2)(beside_2)
        pl.when(i == 3)(beside_3)
        pl.when(i == 4)(beside_4)
        pl.when(i == 5)(beside_5)
        pl.when(i == 6)(beside_6)

    combine(4)
    for c in range(len(own)):
        settle(rows, out_chunks[c], zs.at[c])
        settle(zb, out_chunks[c], ys.at[c])
        arrived(xg.at[x, :, own[c]], xs.at[0, c])
        arrived(xg.at[x, :, own[c]], xs.at[1, c])
        arrived(xg.at[left, top, own[c]], xs.at[2, c])
        arrived(xg.at[right, low, own[c]], xs.at[3, c])
    for c in range(len(cols)):
        settle(cy, cols[c], cys.at[c])
        settle(cz, cols[c], czs.at[c])
        arrived(part_far.at[top, cols[c]], rs.at[0, c])
        arrived(part_far.at[low, cols[c]], rs.at[1, c])
        arrived(near_right.at[low, cols[c]], rs.at[2, c])
        arrived(near_left.at[top, cols[c]], rs.at[3, c])
        arrived(near_right.at[top, cols[c]], rs.at[4, c])
        arrived(near_left.at[low, cols[c]], rs.at[5, c])
    for c in range(PAGE_PARTS):
        settle(ps, page_chunks[c], pzs.at[c])
        settle(pzb, page_chunks[c], pys.at[c])
        arrived(kg.at[x, :, page_chunks[c]], pxs.at[0, c])
        arrived(kg.at[x, :, page_chunks[c]], pxs.at[1, c])
        arrived(kg.at[left, 0:32, page_chunks[c]], pxs.at[2, c])
        arrived(kg.at[right, 32:64, page_chunks[c]], pxs.at[3, c])


def on_device(
    queries,
    suffix_latent,
    page_pool,
    page_owner,
    page_slot,
    prefix_len,
    moe_input,
    expert_ids,
    gate_weights,
    w_gate,
    w_up,
    w_down,
):
    bf, f32 = jnp.bfloat16, jnp.float32
    hid, unit = w_gate.shape[1:]
    wide = page_pool.shape[1] // (2 * NX)
    vmem = pl.BlockSpec(memory_space=pltpu.VMEM)
    hbm = pl.BlockSpec(memory_space=pltpu.HBM)
    dma = pltpu.SemaphoreType.DMA
    d, p, n = len(DISPATCH), PAGE_PARTS, len(COMBINE)
    new, heads = queries.shape[0], queries.shape[1] // KD
    full, paged = pltpu.VMEM((ROWS, hid), bf), pltpu.VMEM((ROWS, wide), bf)
    asking = pltpu.VMEM((ROWS, REQ + hid), bf)
    return pl.pallas_call(
        whole_kernel,
        out_shape=(
            pltpu.VMEM((new, heads * LATENT), bf),
            pltpu.VMEM(moe_input.shape, bf),
        ),
        in_specs=[pl.BlockSpec(memory_space=pltpu.SMEM)] + [vmem] * 5 + [hbm] * 5 + [vmem],
        out_specs=(vmem, vmem),
        scratch_shapes=[
            asking, asking, asking,
            pltpu.VMEM((NX, ROWS, REQ + hid), bf),
            pltpu.VMEM((2, page_pool.shape[0], wide), bf),
            paged, paged, paged, paged,
            pltpu.VMEM((NX, 64, wide), bf),
            pltpu.VMEM((hid, unit), bf), pltpu.VMEM((hid, unit), bf), pltpu.VMEM((unit, hid), bf),
            pltpu.VMEM((NX, ROWS, unit), bf),
            pltpu.VMEM(queries.shape, bf),
            pltpu.VMEM((2048, 640), bf),
            pltpu.VMEM((2176, 640), bf),
            pltpu.VMEM((256, 128), f32),
            full, pltpu.VMEM((ROWS, hid), f32), pltpu.VMEM((ROWS, hid), f32), full, full, pltpu.VMEM((ROWS, hid), f32),
            pltpu.VMEM((64, hid), bf), pltpu.VMEM((64, hid), bf), full, full,
            full, full, full, full,
            dma((6,)),
            dma((d,)), dma((d,)), dma((d,)), dma((d,)), dma((4, d)), dma((4, d)),
            dma((p,)), dma((p,)), dma((p,)), dma((p,)), dma((4, p)), dma((4, p)),
            dma((6, n)), dma((6, n)), dma((n,)), dma((n,)), dma((n,)), dma((n,)),
        ],
        compiler_params=pltpu.CompilerParams(
            collective_id=0, has_side_effects=True, vmem_limit_bytes=52 * 2**20
        ),
        name="whole",
    )(
        prefix_len, expert_ids.T, gate_weights.T, page_owner, page_slot, moe_input,
        page_pool, w_gate, w_up, w_down, queries, suffix_latent.T,
    )


def solution(mesh):
    return jax.shard_map(
        on_device,
        mesh=mesh,
        in_specs=(
            P("ep", "dp"),
            P("ep", None),
            P("ep", None),
            P("ep", None),
            P("ep", None),
            P("ep"),
            P(("dp", "ep"), None),
            P(("dp", "ep"), None),
            P(("dp", "ep"), None),
            P("ep", None, "dp"),
            P("ep", None, "dp"),
            P("ep", "dp", None),
        ),
        out_specs=(P("ep", "dp"), P(("dp", "ep"), None)),
        check_vma=False,
    )
```

```python
import math

import jax
import jax.numpy as jnp
from jax import lax
from jax.experimental import pallas as pl
from jax.experimental.pallas import tpu as pltpu
from jax.sharding import PartitionSpec as P

LATENT = 512
KD = 576
PAGE = 64
SCALE = 0.07216878364870322
NEG = -1e30
LOG2E = 1.4426950408889634

NX = 4
NZ = 8
NG = 8
ROWS = 128
BLOCK = 16
REQ = 128
DISPATCH = (512, 512, 512, 1024, 1024)
PAGES = (1152, 1152, 1152, 1152)
FIRST = 6
COMBINE = (1024, 1024, 768, 512, 256)
MESH = pl.DeviceIdType.MESH


def position():
    x = lax.axis_index("dp")
    ep = lax.axis_index("ep")
    core = lax.rem(ep, 2)
    z = lax.rem(lax.div(ep, 2), NZ)
    y = lax.div(ep, 2 * NZ)
    return x, y, z, core


def peers():
    x, y, z, core = position()
    g = y * 2 + core

    def along_z(d):
        other = lax.rem(z + d, NZ)
        return other, (x, (y * NZ + other) * 2 + core)

    def along_g(d):
        other = lax.rem(g + d, NG)
        return other, (x, (lax.div(other, 2) * NZ + z) * 2 + lax.rem(other, 2))

    def along_x(d):
        other = lax.rem(x + d, NX)
        return other, (other, (y * NZ + z) * 2 + core)

    return (x, z, g), (along_x, along_z, along_g)


def greet(along_x, along_z, along_g):
    barrier = pltpu.get_barrier_semaphore()

    def signal(dev):
        pl.semaphore_signal(barrier, inc=1, device_id=dev, device_id_type=MESH)

    def one(d, carry):
        signal(along_z(d)[1])
        signal(along_g(d)[1])
        return carry

    lax.fori_loop(1, 8, one, 0)
    signal(along_x(1)[1])
    signal(along_x(3)[1])
    return lambda: pl.semaphore_wait(barrier, 16)


def block_at(i):
    return pl.ds(pl.multiple_of(i * BLOCK, BLOCK), BLOCK)


def exchange(src, dst, cols, me, along, send_sem, recv_sem):
    def one(d, carry):
        other, dev = along(d)
        pltpu.make_async_remote_copy(
            src_ref=src.at[block_at(other), cols],
            dst_ref=dst.at[block_at(me), cols],
            send_sem=send_sem,
            recv_sem=recv_sem,
            device_id=dev,
            device_id_type=MESH,
        ).start()
        return carry

    lax.fori_loop(1, 8, one, 0)
    dst[block_at(me), cols] = src[block_at(me), cols]


def settle(ref, cols, sem):
    seven = ref.at[0 : 7 * BLOCK, cols]
    pltpu.make_async_copy(seven, seven, sem).wait()


def send(src, dst, send_sem, recv_sem, dev):
    copy = pltpu.make_async_remote_copy(
        src_ref=src, dst_ref=dst, send_sem=send_sem, recv_sem=recv_sem, device_id=dev, device_id_type=MESH
    )
    copy.start()
    return copy


def arrived(ref, sem):
    pltpu.make_async_copy(ref, ref, sem).wait()


def regroup():
    to = lax.broadcasted_iota(jnp.int32, (ROWS, ROWS), 0)
    of = lax.broadcasted_iota(jnp.int32, (ROWS, ROWS), 1)
    wanted = (lax.rem(to, 16) >> 1) * 16 + (to >> 4) * 2 + (to & 1)
    return jnp.where(of == wanted, 1.0, 0.0).astype(jnp.bfloat16)


def mm(a, b):
    return jnp.dot(a, b, preferred_element_type=jnp.float32)


def nt(a, b):
    return lax.dot_general(a, b, (((1,), (1,)), ((), ())), preferred_element_type=jnp.float32)


def iota(shape, dim):
    return lax.broadcasted_iota(jnp.int32, shape, dim)


def device_of(outer, inner, z_first):
    z, g = (outer, inner) if z_first else (inner, outer)
    return ((g >> 1) * NZ + z) * 2 + (g & 1)


def row_device(shape, dim, z_first):
    row = iota(shape, dim)
    return device_of(row >> 4, (row >> 1) & 7, z_first)


def identity(size):
    return jnp.where(iota((size, size), 0) == iota((size, size), 1), 1.0, 0.0).astype(jnp.bfloat16)


def spans(sizes, start=0):
    found = []
    for size in sizes:
        found.append(slice(start, start + size))
        start += size
    return found


def whole_kernel(
    length, ids, gates, owner, slot, tokens, pool_hbm, wg_hbm, wu_hbm, wd_hbm, q_hbm, suffix,
    context, out,
    rows, za, zb, xg, pool, ps, pza, pzb, pya, kg, wg, wu, wd, hidden,
    queries, qx, keys, causal, partial, stats,
    part_far, part_right, part_left, near_right, near_left, part_own, relay_left, relay_right, from_left, from_right,
    cy, cya, cz, cza,
    local, zs, zr, ys, yr, xs, xr, pzs, pzr, pys, pyr, pxs, pxr, rs, rr, cys, cyr, czs, czr,
):
    (x, z, g), (along_x, along_z, along_g) = peers()
    greeted = greet(along_x, along_z, along_g)
    bf, f32 = jnp.bfloat16, jnp.float32
    half_page = pool.shape[2]
    loads = [
        pltpu.make_async_copy(
            pool_hbm.at[:, pl.ds(pl.multiple_of(x * (2 * half_page) + i * half_page, 128), half_page)],
            pool.at[i],
            local.at[i],
        )
        for i in range(2)
    ]
    loads += [
        pltpu.make_async_copy(wg_hbm.at[0], wg, local.at[2]),
        pltpu.make_async_copy(wu_hbm.at[0], wu, local.at[3]),
        pltpu.make_async_copy(wd_hbm.at[0], wd, local.at[4]),
        pltpu.make_async_copy(q_hbm, queries, local.at[5]),
    ]
    for load in loads:
        load.start()
    tok_count, hid = tokens.shape
    own = spans((DISPATCH[0], *DISPATCH[2:], DISPATCH[1]))
    own = [own[0], own[-1], *own[1:-1]]
    out_chunks = [own[0], slice(own[1].start, hid + REQ), *own[2:]]
    page_chunks = spans(PAGES)
    firsts = next(i for i in range(len(PAGES) + 1) if sum(PAGES[:i]) >= FIRST * KD)
    cols = spans(COMBINE)
    right, to_right = along_x(1)
    left, to_left = along_x(3)
    far = lax.rem(x + 2, NX)
    mine = xg.at[x]
    perm = regroup()
    top, low = slice(0, 64), slice(64, 128)

    expert = row_device((ROWS, tok_count), 0, True)
    hits = [ids[k : k + 1, :] == expert for k in range(ids.shape[0])]
    named = hits[0]
    for hit in hits[1:]:
        named = named | hit
    below = (iota((tok_count, tok_count), 0) < iota((tok_count, tok_count), 1)).astype(f32).astype(bf)
    before = mm(named.astype(f32).astype(bf), below)
    placed = named & (before == (iota((ROWS, tok_count), 0) & 1).astype(f32))
    page_count = owner.shape[1]
    asks = owner[...] == row_device((ROWS, page_count), 0, True)
    asked = jnp.sum(jnp.where(asks, slot[...] + 1, 0), axis=1, keepdims=True)
    lane = iota((ROWS, REQ), 1)
    row = iota((ROWS, REQ), 0)
    req = (lane < 16) & ((lane & 7) + 1 == asked) & ((lane >> 3) == (row & 1))
    rows[:, hid:] = req.astype(f32).astype(bf)
    rows[:, 0:hid] = mm(placed.astype(f32).astype(bf), tokens[...]).astype(bf)
    greeted()
    for c in range(len(out_chunks)):
        exchange(rows, za, out_chunks[c], z, along_z, zs.at[0], zr.at[c])

    weight = jnp.zeros((ROWS, tok_count), f32)
    for k, hit in enumerate(hits):
        weight = weight + jnp.where(hit & placed, gates[k : k + 1, :], 0.0)
    gate_1 = weight.astype(bf)
    rest = weight - gate_1.astype(f32)
    gate_2 = rest.astype(bf)
    gate_3 = (rest - gate_2.astype(f32)).astype(bf)
    eye = identity(tok_count)
    gate_1, gate_2, gate_3 = (nt(eye, part).astype(bf) for part in (gate_1, gate_2, gate_3))
    holds = (owner[...] == row_device((ROWS, page_count), 0, False)).astype(f32).astype(bf)
    spread = ((iota((64, page_count), 0) >> 1) == iota((64, page_count), 1)).astype(f32).astype(bf)
    sel = jnp.where((iota((64, ROWS), 0) & 1) == (iota((64, ROWS), 1) & 1), nt(spread, holds), 0.0).astype(bf)

    def z_to_y(c):
        settle(za, out_chunks[c], zr.at[c])
        zb[:, out_chunks[c]] = mm(perm, za[:, out_chunks[c]]).astype(bf)
        exchange(zb, mine, out_chunks[c], g, along_g, ys.at[0], yr.at[c])

    def y_to_x(c):
        settle(mine, out_chunks[c], yr.at[c])
        part = xg.at[x, :, own[c]]
        send(part, part, xs.at[0], xr.at[0, c], to_right)
        send(part, part, xs.at[1], xr.at[1, c], to_left)

    def forward(c):
        arrived(xg.at[left, :, own[c]], xr.at[0, c])
        part = xg.at[left, top, own[c]]
        send(part, part, xs.at[2], xr.at[2, 0], to_right)
        arrived(xg.at[right, :, own[c]], xr.at[1, c])
        part = xg.at[right, low, own[c]]
        send(part, part, xs.at[3], xr.at[2, 0], to_left)

    def ask():
        wanted = mm(perm, xg[x, :, hid:]).astype(bf)
        loads[0].wait()
        loads[1].wait()
        for c in range(len(PAGES)):
            ps[:, page_chunks[c]] = (
                mm(wanted[:, 0:8], pool[0, :, page_chunks[c]]) + mm(wanted[:, 8:16], pool[1, :, page_chunks[c]])
            ).astype(bf)
            exchange(ps, pza, page_chunks[c], z, along_z, pzs.at[0], pzr.at[c])

    def page_z_to_y(c):
        settle(pza, page_chunks[c], pzr.at[c])
        pzb[:, page_chunks[c]] = mm(perm, pza[:, page_chunks[c]]).astype(bf)
        exchange(pzb, pya, page_chunks[c], g, along_g, pys.at[0], pyr.at[c])

    def page_y_to_x(c):
        settle(pya, page_chunks[c], pyr.at[c])
        kg[x, :, page_chunks[c]] = mm(sel, pya[:, page_chunks[c]]).astype(bf)
        part = kg.at[x, :, page_chunks[c]]
        send(part, part, pxs.at[0], pxr.at[0, c], to_right)
        send(part, part, pxs.at[1], pxr.at[1, c], to_left)

    def page_forward(c):
        arrived(kg.at[left, :, page_chunks[c]], pxr.at[0, c])
        part = kg.at[left, 0:32, page_chunks[c]]
        send(part, part, pxs.at[2], pxr.at[2, c], to_right)
        arrived(kg.at[right, :, page_chunks[c]], pxr.at[1, c])
        part = kg.at[right, 32:64, page_chunks[c]]
        send(part, part, pxs.at[3], pxr.at[2, c], to_left)

    def ffn(group):
        taken = xg[group, :, 0:hid]
        gate = mm(taken, wg[...])
        up = mm(taken, wu[...])
        hidden[group] = (gate / (1.0 + jnp.exp(-gate)) * up).astype(bf)

    def calc_far(c):
        part_far[:, cols[c]] = mm(hidden[far], wd[:, cols[c]]).astype(bf)

    def calc_near(c):
        part_right[:, cols[c]] = mm(hidden[right], wd[:, cols[c]])
        part_left[:, cols[c]] = mm(hidden[left], wd[:, cols[c]])
        near_right[low, cols[c]] = part_right[low, cols[c]].astype(bf)
        near_left[top, cols[c]] = part_left[top, cols[c]].astype(bf)
        part_own[:, cols[c]] = mm(hidden[x], wd[:, cols[c]])

    def start_far(c):
        send(part_far.at[top, cols[c]], relay_left.at[:, cols[c]], rs.at[0], rr.at[0, c], to_right)
        send(part_far.at[low, cols[c]], relay_right.at[:, cols[c]], rs.at[1], rr.at[1, c], to_left)

    def start_near(c):
        send(near_right.at[low, cols[c]], from_left.at[low, cols[c]], rs.at[2], rr.at[2, c], to_right)
        send(near_left.at[top, cols[c]], from_right.at[top, cols[c]], rs.at[3], rr.at[3, c], to_left)

    def relay(c):
        arrived(relay_left.at[:, cols[c]], rr.at[0, c])
        near_right[top, cols[c]] = (part_right[top, cols[c]] + relay_left[:, cols[c]].astype(f32)).astype(bf)
        send(near_right.at[top, cols[c]], from_left.at[top, cols[c]], rs.at[4], rr.at[2, c], to_right)
        arrived(relay_right.at[:, cols[c]], rr.at[1, c])
        near_left[low, cols[c]] = (part_left[low, cols[c]] + relay_right[:, cols[c]].astype(f32)).astype(bf)
        send(near_left.at[low, cols[c]], from_right.at[low, cols[c]], rs.at[5], rr.at[3, c], to_left)

    def to_y(c):
        arrived(from_left.at[:, cols[c]], rr.at[2, c])
        arrived(from_right.at[:, cols[c]], rr.at[3, c])
        cy[:, cols[c]] = (
            part_own[:, cols[c]] + from_left[:, cols[c]].astype(f32) + from_right[:, cols[c]].astype(f32)
        ).astype(bf)
        exchange(cy, cya, cols[c], g, along_g, cys.at[0], cyr.at[c])

    def to_z(c):
        settle(cya, cols[c], cyr.at[c])
        cz[:, cols[c]] = mm(perm, cya[:, cols[c]]).astype(bf)
        exchange(cz, cza, cols[c], z, along_z, czs.at[0], czr.at[c])

    def combine(c):
        settle(cza, cols[c], czr.at[c])
        back = cza[:, cols[c]]
        out[:, cols[c]] = (mm(gate_1, back) + mm(gate_2, back) + mm(gate_3, back)).astype(bf)

    def place_queries():
        loads[5].wait()
        one = jnp.where(iota((128, 64), 1) == 0, 1.0, 0.0).astype(bf)
        for h in range(16):
            qx[h * 128 : (h + 1) * 128, 0:KD] = queries[:, h * KD : (h + 1) * KD]
            qx[h * 128 : (h + 1) * 128, KD : KD + 64] = one
        causal[...] = jnp.where(iota((256, 128), 1) > (iota((256, 128), 0) & 127), NEG, 0.0)
        keys[2048:2176, 0:KD] = nt(identity(128), suffix[...]).astype(bf)
        keys[2048:2176, KD : KD + 64] = jnp.zeros((128, 64), bf)

    def gather_keys(begin, end):
        lanes, line = iota((64, 64), 1), iota((64, 64), 0)
        for j in range(begin, end):
            for q in range(4):
                at = slice((j * 4 + q) * 64, (j * 4 + q + 1) * 64)
                keys[at, 0:KD] = kg[q, :, j * KD : (j + 1) * KD]
                place = (line >> 1) * PAGE + q * 16 + (line & 1) * 8 + j
                keys[at, KD : KD + 64] = jnp.where((lanes == 0) & (place >= length[0]), NEG, 0.0).astype(bf)

    split = FIRST * 256
    tempo = SCALE * LOG2E

    def attend_first(i):
        at = pl.ds(pl.multiple_of(i * 256, 256), 256)
        q = qx[at, :]
        near = nt(q, keys[2048:2176, :]) + causal[...]
        past = nt(q, keys[0:split, :])
        peak = jnp.maximum(jnp.max(past, axis=1, keepdims=True), jnp.max(near, axis=1, keepdims=True)) * tempo
        past = jnp.exp2(past * tempo - peak)
        near = jnp.exp2(near * tempo - peak)
        stats[at, 0:1] = peak
        stats[at, 1:2] = jnp.sum(past, axis=1, keepdims=True) + jnp.sum(near, axis=1, keepdims=True)
        partial[at, :] = mm(past.astype(bf), keys[0:split, 0:LATENT]) + mm(
            near.astype(bf), keys[2048:2176, 0:LATENT]
        )

    def attend_second(i):
        at = pl.ds(pl.multiple_of(i * 256, 256), 256)
        q = qx[at, :]
        past = nt(q, keys[split:2048, :])
        was = stats[at, 0:1]
        peak = jnp.maximum(jnp.max(past, axis=1, keepdims=True) * tempo, was)
        past = jnp.exp2(past * tempo - peak)
        fade = jnp.exp2(was - peak)
        total = stats[at, 1:2] * fade + jnp.sum(past, axis=1, keepdims=True)
        got = mm(past.astype(bf), keys[split:2048, 0:LATENT]) + partial[at, :] * fade
        got = (got / total).astype(bf)
        to = pl.multiple_of(i * 1024, 1024)
        context[:, pl.ds(to, 512)] = got[0:128]
        context[:, pl.ds(to + 512, 512)] = got[128:256]

    def wait_far():
        arrived(xg.at[far, :, 0:hid], xr.at[2, 0])

    def wait_keys(begin, end):
        for c in range(begin, end):
            arrived(kg.at[far, :, page_chunks[c]], pxr.at[2, c])

    def wait_weights():
        for i in (2, 3, 4):
            loads[i].wait()

    def drain_dispatch():
        settle(rows, slice(0, hid + REQ), zs.at[0])
        settle(zb, slice(0, hid + REQ), ys.at[0])
        arrived(xg.at[x, :, 0:hid], xs.at[0])
        arrived(xg.at[x, :, 0:hid], xs.at[1])
        arrived(xg.at[left, top, 0:hid], xs.at[2])
        arrived(xg.at[right, low, 0:hid], xs.at[3])
        settle(ps, slice(0, half_page), pzs.at[0])

    def drain():
        settle(pzb, slice(0, half_page), pys.at[0])
        arrived(kg.at[x], pxs.at[0])
        arrived(kg.at[x], pxs.at[1])
        arrived(kg.at[left, 0:32], pxs.at[2])
        arrived(kg.at[right, 32:64], pxs.at[3])
        arrived(part_far.at[top], rs.at[0])
        arrived(part_far.at[low], rs.at[1])
        arrived(near_right.at[low], rs.at[2])
        arrived(near_left.at[top], rs.at[3])
        arrived(near_right.at[top], rs.at[4])
        arrived(near_left.at[low], rs.at[5])
        settle(cy, slice(0, hid), cys.at[0])
        settle(cz, slice(0, hid), czs.at[0])

    z_to_y(0)
    z_to_y(1)
    y_to_x(0)
    z_to_y(2)
    y_to_x(1)
    y_to_x(2)
    forward(0)
    z_to_y(3)
    forward(1)
    ask()
    forward(2)
    y_to_x(3)
    z_to_y(4)
    place_queries()
    y_to_x(4)
    forward(3)
    wait_weights()
    ffn(x)
    page_z_to_y(0)
    page_z_to_y(1)
    forward(4)
    ffn(right)
    page_y_to_x(0)
    ffn(left)
    page_z_to_y(2)
    page_y_to_x(1)
    wait_far()
    page_forward(0)
    ffn(far)
    calc_far(0)
    page_y_to_x(2)
    start_far(0)
    calc_near(0)
    calc_far(1)
    page_forward(1)
    calc_near(1)
    page_z_to_y(3)
    calc_far(2)
    page_forward(2)
    calc_near(2)
    calc_near(3)
    start_far(1)
    start_near(0)
    calc_far(3)
    relay(0)
    drain_dispatch()
    wait_keys(0, firsts)
    start_near(1)
    gather_keys(0, FIRST)
    def first_0():
        calc_near(4)
        relay(1)
        start_far(2)

    def first_1():
        start_near(2)

    def first_3():
        to_y(0)
        start_far(3)

    def first_5():
        to_y(1)
        start_near(3)
        to_z(0)
        calc_far(4)
        relay(2)

    def first_6():
        start_far(4)
        relay(3)
        page_y_to_x(3)
        start_near(4)
        to_z(1)
        to_y(2)
        relay(4)
        to_y(3)

    @pl.loop(0, 8)
    def _(i):
        attend_first(i)
        pl.when(i == 0)(first_0)
        pl.when(i == 1)(first_1)
        pl.when(i == 3)(first_3)
        pl.when(i == 5)(first_5)
        pl.when(i == 6)(first_6)

    page_forward(3)
    to_z(2)
    combine(0)
    to_y(4)
    to_z(3)
    combine(1)
    wait_keys(firsts, len(PAGES))
    gather_keys(FIRST, 8)
    def second_1():
        to_z(4)

    def second_4():
        combine(2)

    @pl.loop(0, 8)
    def _(i):
        attend_second(i)
        pl.when(i == 1)(second_1)
        pl.when(i == 4)(second_4)

    combine(3)
    combine(4)
    drain()


def on_device(
    queries,
    suffix_latent,
    page_pool,
    page_owner,
    page_slot,
    prefix_len,
    moe_input,
    expert_ids,
    gate_weights,
    w_gate,
    w_up,
    w_down,
):
    bf, f32 = jnp.bfloat16, jnp.float32
    hid, unit = w_gate.shape[1:]
    wide = page_pool.shape[1] // (2 * NX)
    vmem = pl.BlockSpec(memory_space=pltpu.VMEM)
    hbm = pl.BlockSpec(memory_space=pltpu.HBM)
    dma = pltpu.SemaphoreType.DMA
    d, p, n = len(DISPATCH), len(PAGES), len(COMBINE)
    new, heads = queries.shape[0], queries.shape[1] // KD
    full, paged = pltpu.VMEM((ROWS, hid), bf), pltpu.VMEM((ROWS, wide), bf)
    asking = pltpu.VMEM((ROWS, REQ + hid), bf)
    return pl.pallas_call(
        whole_kernel,
        out_shape=(
            pltpu.VMEM((new, heads * LATENT), bf),
            pltpu.VMEM(moe_input.shape, bf),
        ),
        in_specs=[pl.BlockSpec(memory_space=pltpu.SMEM)] + [vmem] * 5 + [hbm] * 5 + [vmem],
        out_specs=(vmem, vmem),
        scratch_shapes=[
            asking, asking, asking,
            pltpu.VMEM((NX, ROWS, REQ + hid), bf),
            pltpu.VMEM((2, page_pool.shape[0], wide), bf),
            paged, paged, paged, paged,
            pltpu.VMEM((NX, 64, wide), bf),
            pltpu.VMEM((hid, unit), bf), pltpu.VMEM((hid, unit), bf), pltpu.VMEM((unit, hid), bf),
            pltpu.VMEM((NX, ROWS, unit), bf),
            pltpu.VMEM(queries.shape, bf),
            pltpu.VMEM((2048, 640), bf),
            pltpu.VMEM((2176, 640), bf),
            pltpu.VMEM((256, 128), f32),
            pltpu.VMEM((2048, LATENT), f32),
            pltpu.VMEM((2048, 128), f32),
            full, pltpu.VMEM((ROWS, hid), f32), pltpu.VMEM((ROWS, hid), f32), full, full, pltpu.VMEM((ROWS, hid), f32),
            pltpu.VMEM((64, hid), bf), pltpu.VMEM((64, hid), bf), full, full,
            full, full, full, full,
            dma((6,)),
            dma((1,)), dma((d,)), dma((1,)), dma((d,)), dma((4,)), dma((3, d)),
            dma((1,)), dma((p,)), dma((1,)), dma((p,)), dma((4,)), dma((3, p)),
            dma((6,)), dma((4, n)), dma((1,)), dma((n,)), dma((1,)), dma((n,)),
        ],
        compiler_params=pltpu.CompilerParams(
            collective_id=0, has_side_effects=True, vmem_limit_bytes=54 * 2**20
        ),
        name="whole",
    )(
        prefix_len, expert_ids.T, gate_weights.T, page_owner, page_slot, moe_input,
        page_pool, w_gate, w_up, w_down, queries, suffix_latent.T,
    )


def solution(mesh):
    return jax.shard_map(
        on_device,
        mesh=mesh,
        in_specs=(
            P("ep", "dp"),
            P("ep", None),
            P("ep", None),
            P("ep", None),
            P("ep", None),
            P("ep"),
            P(("dp", "ep"), None),
            P(("dp", "ep"), None),
            P(("dp", "ep"), None),
            P("ep", None, "dp"),
            P("ep", None, "dp"),
            P("ep", "dp", None),
        ),
        out_specs=(P("ep", "dp"), P(("dp", "ep"), None)),
        check_vma=False,
    )
```

```python
import math

import jax
import jax.numpy as jnp
from jax import lax
from jax.experimental import pallas as pl
from jax.experimental.pallas import tpu as pltpu
from jax.sharding import PartitionSpec as P

LATENT = 512
KD = 576
PAGE = 64
SCALE = 0.07216878364870322
NEG = -1e30
LOG2E = 1.4426950408889634

NX = 4
NZ = 8
NG = 8
ROWS = 128
BLOCK = 16
REQ = 128
DISPATCH = (512, 512, 512, 1024, 1024)
PAGES = (1152, 1152, 1152, 1152)
FIRST = 6
COMBINE = (1024, 1024, 768, 512, 256)
MESH = pl.DeviceIdType.MESH


def position():
    x = lax.axis_index("dp")
    ep = lax.axis_index("ep")
    core = lax.rem(ep, 2)
    z = lax.rem(lax.div(ep, 2), NZ)
    y = lax.div(ep, 2 * NZ)
    return x, y, z, core


def peers():
    x, y, z, core = position()
    g = y * 2 + core

    def along_z(d):
        other = lax.rem(z + d, NZ)
        return other, (x, (y * NZ + other) * 2 + core)

    def along_g(d):
        other = lax.rem(g + d, NG)
        return other, (x, (lax.div(other, 2) * NZ + z) * 2 + lax.rem(other, 2))

    def along_x(d):
        other = lax.rem(x + d, NX)
        return other, (other, (y * NZ + z) * 2 + core)

    return (x, z, g), (along_x, along_z, along_g)


def farthest_first(i):
    return 4 + (i >> 1) * (2 * (i & 1) - 1)


def greet(along_x, along_z, along_g):
    barrier = pltpu.get_barrier_semaphore()

    def signal(dev):
        pl.semaphore_signal(barrier, inc=1, device_id=dev, device_id_type=MESH)

    def one(d, carry):
        signal(along_z(farthest_first(d))[1])
        signal(along_g(farthest_first(d))[1])
        return carry

    lax.fori_loop(1, 8, one, 0)
    signal(along_x(1)[1])
    signal(along_x(3)[1])
    return lambda: pl.semaphore_wait(barrier, 16)


def block_at(i):
    return pl.ds(pl.multiple_of(i * BLOCK, BLOCK), BLOCK)


def exchange(src, dst, cols, me, along, send_sem, recv_sem):
    def one(d, carry):
        other, dev = along(farthest_first(d))
        pltpu.make_async_remote_copy(
            src_ref=src.at[block_at(other), cols],
            dst_ref=dst.at[block_at(me), cols],
            send_sem=send_sem,
            recv_sem=recv_sem,
            device_id=dev,
            device_id_type=MESH,
        ).start()
        return carry

    lax.fori_loop(1, 8, one, 0)
    dst[block_at(me), cols] = src[block_at(me), cols]


def settle(ref, cols, sem):
    seven = ref.at[0 : 7 * BLOCK, cols]
    pltpu.make_async_copy(seven, seven, sem).wait()


def send(src, dst, send_sem, recv_sem, dev):
    copy = pltpu.make_async_remote_copy(
        src_ref=src, dst_ref=dst, send_sem=send_sem, recv_sem=recv_sem, device_id=dev, device_id_type=MESH
    )
    copy.start()
    return copy


def arrived(ref, sem):
    pltpu.make_async_copy(ref, ref, sem).wait()


def regroup():
    to = lax.broadcasted_iota(jnp.int32, (ROWS, ROWS), 0)
    of = lax.broadcasted_iota(jnp.int32, (ROWS, ROWS), 1)
    wanted = (lax.rem(to, 16) >> 1) * 16 + (to >> 4) * 2 + (to & 1)
    return jnp.where(of == wanted, 1.0, 0.0).astype(jnp.bfloat16)


def mm(a, b):
    return jnp.dot(a, b, preferred_element_type=jnp.float32)


def nt(a, b):
    return lax.dot_general(a, b, (((1,), (1,)), ((), ())), preferred_element_type=jnp.float32)


def iota(shape, dim):
    return lax.broadcasted_iota(jnp.int32, shape, dim)


def device_of(outer, inner, z_first):
    z, g = (outer, inner) if z_first else (inner, outer)
    return ((g >> 1) * NZ + z) * 2 + (g & 1)


def row_device(shape, dim, z_first):
    row = iota(shape, dim)
    return device_of(row >> 4, (row >> 1) & 7, z_first)


def identity(size):
    return jnp.where(iota((size, size), 0) == iota((size, size), 1), 1.0, 0.0).astype(jnp.bfloat16)


def spans(sizes, start=0):
    found = []
    for size in sizes:
        found.append(slice(start, start + size))
        start += size
    return found


def whole_kernel(
    length, ids_hbm, gates_hbm, owner_hbm, slot_hbm, tokens_hbm, pool_hbm, wg_hbm, wu_hbm, wd_hbm, q_hbm, suffix_hbm,
    context, out,
    ids, gates, owner, slot, tokens, suffix,
    rows, za, zb, xg, pool, ps, pza, pzb, pya, kg, wg, wu, wd, hidden,
    queries, qx, keys, causal, partial, stats,
    part_far, part_right, part_left, near_right, near_left, part_own, relay_left, relay_right, from_left, from_right,
    cy, cya, cz, cza,
    local, zs, zr, ys, yr, xs, xr, pzs, pzr, pys, pyr, pxs, pxr, rs, rr, cys, cyr, czs, czr,
):
    (x, z, g), (along_x, along_z, along_g) = peers()
    greeted = greet(along_x, along_z, along_g)
    bf, f32 = jnp.bfloat16, jnp.float32
    small = [
        pltpu.make_async_copy(src, dst, local.at[6 + i])
        for i, (src, dst) in enumerate(
            ((ids_hbm, ids), (tokens_hbm, tokens), (owner_hbm, owner), (slot_hbm, slot), (gates_hbm, gates), (suffix_hbm, suffix))
        )
    ]
    for load in small:
        load.start()
    half_page = pool.shape[2]
    loads = [
        pltpu.make_async_copy(
            pool_hbm.at[:, pl.ds(pl.multiple_of(x * (2 * half_page) + i * half_page, 128), half_page)],
            pool.at[i],
            local.at[i],
        )
        for i in range(2)
    ]
    loads += [
        pltpu.make_async_copy(wg_hbm.at[0], wg, local.at[2]),
        pltpu.make_async_copy(wu_hbm.at[0], wu, local.at[3]),
        pltpu.make_async_copy(wd_hbm.at[0], wd, local.at[4]),
        pltpu.make_async_copy(q_hbm, queries, local.at[5]),
    ]
    for load in loads:
        load.start()
    tok_count, hid = tokens.shape
    own = spans((DISPATCH[0], *DISPATCH[2:], DISPATCH[1]))
    own = [own[0], own[-1], *own[1:-1]]
    out_chunks = [own[0], slice(own[1].start, hid + REQ), *own[2:]]
    page_chunks = spans(PAGES)
    firsts = next(i for i in range(len(PAGES) + 1) if sum(PAGES[:i]) >= FIRST * KD)
    cols = spans(COMBINE)
    right, to_right = along_x(1)
    left, to_left = along_x(3)
    far = lax.rem(x + 2, NX)
    mine = xg.at[x]
    perm = regroup()
    top, low = slice(0, 64), slice(64, 128)

    small[0].wait()
    expert = row_device((ROWS, tok_count), 0, True)
    hits = [ids[k : k + 1, :] == expert for k in range(ids.shape[0])]
    named = hits[0]
    for hit in hits[1:]:
        named = named | hit
    below = (iota((tok_count, tok_count), 0) < iota((tok_count, tok_count), 1)).astype(f32).astype(bf)
    before = mm(named.astype(f32).astype(bf), below)
    placed = named & (before == (iota((ROWS, tok_count), 0) & 1).astype(f32))
    placing = placed.astype(f32).astype(bf)
    small[1].wait()

    def z_send(c):
        rows[:, own[c]] = mm(placing, tokens[:, own[c]]).astype(bf)
        exchange(rows, za, out_chunks[c], z, along_z, zs.at[0], zr.at[c])

    greeted()
    z_send(0)
    page_count = owner.shape[1]
    small[2].wait()
    small[3].wait()
    asks = owner[...] == row_device((ROWS, page_count), 0, True)
    asked = jnp.sum(jnp.where(asks, slot[...] + 1, 0), axis=1, keepdims=True)
    lane = iota((ROWS, REQ), 1)
    row = iota((ROWS, REQ), 0)
    req = (lane < 16) & ((lane & 7) + 1 == asked) & ((lane >> 3) == (row & 1))
    rows[:, hid:] = req.astype(f32).astype(bf)
    for c in range(1, len(own)):
        z_send(c)

    small[4].wait()
    small[5].wait()
    weight = jnp.zeros((ROWS, tok_count), f32)
    for k, hit in enumerate(hits):
        weight = weight + jnp.where(hit & placed, gates[k : k + 1, :], 0.0)
    gate_1 = weight.astype(bf)
    rest = weight - gate_1.astype(f32)
    gate_2 = rest.astype(bf)
    gate_3 = (rest - gate_2.astype(f32)).astype(bf)
    eye = identity(tok_count)
    gate_parts = jnp.concatenate([nt(eye, part) for part in (gate_1, gate_2, gate_3)], axis=0).astype(bf)
    holds = (owner[...] == row_device((ROWS, page_count), 0, False)).astype(f32).astype(bf)
    spread = ((iota((64, page_count), 0) >> 1) == iota((64, page_count), 1)).astype(f32).astype(bf)
    sel = jnp.where((iota((64, ROWS), 0) & 1) == (iota((64, ROWS), 1) & 1), nt(spread, holds), 0.0).astype(bf)

    def z_to_y(c):
        settle(za, out_chunks[c], zr.at[c])
        zb[:, out_chunks[c]] = mm(perm, za[:, out_chunks[c]]).astype(bf)
        exchange(zb, mine, out_chunks[c], g, along_g, ys.at[0], yr.at[c])

    def y_to_x(c):
        settle(mine, out_chunks[c], yr.at[c])
        part = xg.at[x, :, own[c]]
        send(part, part, xs.at[0], xr.at[0, c], to_right)
        send(part, part, xs.at[1], xr.at[1, c], to_left)

    def forward(c):
        arrived(xg.at[left, :, own[c]], xr.at[0, c])
        part = xg.at[left, top, own[c]]
        send(part, part, xs.at[2], xr.at[2, 0], to_right)
        arrived(xg.at[right, :, own[c]], xr.at[1, c])
        part = xg.at[right, low, own[c]]
        send(part, part, xs.at[3], xr.at[2, 0], to_left)

    def ask():
        wanted = mm(perm, xg[x, :, hid:]).astype(bf)
        loads[0].wait()
        loads[1].wait()
        for c in range(len(PAGES)):
            ps[:, page_chunks[c]] = (
                mm(wanted[:, 0:8], pool[0, :, page_chunks[c]]) + mm(wanted[:, 8:16], pool[1, :, page_chunks[c]])
            ).astype(bf)
            exchange(ps, pza, page_chunks[c], z, along_z, pzs.at[0], pzr.at[c])

    def page_z_to_y(c):
        settle(pza, page_chunks[c], pzr.at[c])
        pzb[:, page_chunks[c]] = mm(perm, pza[:, page_chunks[c]]).astype(bf)
        exchange(pzb, pya, page_chunks[c], g, along_g, pys.at[0], pyr.at[c])

    def page_y_to_x(c):
        settle(pya, page_chunks[c], pyr.at[c])
        kg[x, :, page_chunks[c]] = mm(sel, pya[:, page_chunks[c]]).astype(bf)
        part = kg.at[x, :, page_chunks[c]]
        send(part, part, pxs.at[0], pxr.at[0, c], to_right)
        send(part, part, pxs.at[1], pxr.at[1, c], to_left)

    def page_forward(c):
        arrived(kg.at[left, :, page_chunks[c]], pxr.at[0, c])
        part = kg.at[left, 0:32, page_chunks[c]]
        send(part, part, pxs.at[2], pxr.at[2, c], to_right)
        arrived(kg.at[right, :, page_chunks[c]], pxr.at[1, c])
        part = kg.at[right, 32:64, page_chunks[c]]
        send(part, part, pxs.at[3], pxr.at[2, c], to_left)

    def ffn(group):
        taken = xg[group, :, 0:hid]
        gate = mm(taken, wg[...])
        up = mm(taken, wu[...])
        hidden[group] = (gate / (1.0 + jnp.exp(-gate)) * up).astype(bf)

    def calc_far(c):
        part_far[:, cols[c]] = mm(hidden[far], wd[:, cols[c]]).astype(bf)

    def calc_near(c):
        part_right[:, cols[c]] = mm(hidden[right], wd[:, cols[c]])
        part_left[:, cols[c]] = mm(hidden[left], wd[:, cols[c]])
        near_right[low, cols[c]] = part_right[low, cols[c]].astype(bf)
        near_left[top, cols[c]] = part_left[top, cols[c]].astype(bf)
        part_own[:, cols[c]] = mm(hidden[x], wd[:, cols[c]])

    def start_far(c):
        send(part_far.at[top, cols[c]], relay_left.at[:, cols[c]], rs.at[0], rr.at[0, c], to_right)
        send(part_far.at[low, cols[c]], relay_right.at[:, cols[c]], rs.at[1], rr.at[1, c], to_left)

    def start_near(c):
        send(near_right.at[low, cols[c]], from_left.at[low, cols[c]], rs.at[2], rr.at[2, c], to_right)
        send(near_left.at[top, cols[c]], from_right.at[top, cols[c]], rs.at[3], rr.at[3, c], to_left)

    def relay(c):
        arrived(relay_left.at[:, cols[c]], rr.at[0, c])
        near_right[top, cols[c]] = (part_right[top, cols[c]] + relay_left[:, cols[c]].astype(f32)).astype(bf)
        send(near_right.at[top, cols[c]], from_left.at[top, cols[c]], rs.at[4], rr.at[2, c], to_right)
        arrived(relay_right.at[:, cols[c]], rr.at[1, c])
        near_left[low, cols[c]] = (part_left[low, cols[c]] + relay_right[:, cols[c]].astype(f32)).astype(bf)
        send(near_left.at[low, cols[c]], from_right.at[low, cols[c]], rs.at[5], rr.at[3, c], to_left)

    def to_y(c):
        arrived(from_left.at[:, cols[c]], rr.at[2, c])
        arrived(from_right.at[:, cols[c]], rr.at[3, c])
        cy[:, cols[c]] = (
            part_own[:, cols[c]] + from_left[:, cols[c]].astype(f32) + from_right[:, cols[c]].astype(f32)
        ).astype(bf)
        exchange(cy, cya, cols[c], g, along_g, cys.at[0], cyr.at[c])

    def to_z(c):
        settle(cya, cols[c], cyr.at[c])
        cz[:, cols[c]] = mm(perm, cya[:, cols[c]]).astype(bf)
        exchange(cz, cza, cols[c], z, along_z, czs.at[0], czr.at[c])

    def combine(c):
        settle(cza, cols[c], czr.at[c])
        back = cza[:, cols[c]]
        sums = mm(gate_parts, back)
        n = tok_count
        out[:, cols[c]] = (sums[0:n] + sums[n : 2 * n] + sums[2 * n :]).astype(bf)

    def place_queries():
        loads[5].wait()
        one = jnp.where(iota((128, 64), 1) == 0, 1.0, 0.0).astype(bf)
        for h in range(16):
            qx[h * 128 : (h + 1) * 128, 0:KD] = queries[:, h * KD : (h + 1) * KD]
            qx[h * 128 : (h + 1) * 128, KD : KD + 64] = one
        causal[...] = jnp.where(iota((256, 128), 1) > (iota((256, 128), 0) & 127), NEG, 0.0)
        keys[2048:2176, 0:KD] = nt(identity(128), suffix[...]).astype(bf)
        keys[2048:2176, KD : KD + 64] = jnp.zeros((128, 64), bf)

    def gather_keys(begin, end):
        lanes, line = iota((64, 64), 1), iota((64, 64), 0)
        for j in range(begin, end):
            for q in range(4):
                at = slice((j * 4 + q) * 64, (j * 4 + q + 1) * 64)
                keys[at, 0:KD] = kg[q, :, j * KD : (j + 1) * KD]
                place = (line >> 1) * PAGE + q * 16 + (line & 1) * 8 + j
                keys[at, KD : KD + 64] = jnp.where((lanes == 0) & (place >= length[0]), NEG, 0.0).astype(bf)

    split = FIRST * 256
    tempo = SCALE * LOG2E

    def attend_first(i):
        at = pl.ds(pl.multiple_of(i * 256, 256), 256)
        q = qx[at, :]
        near = nt(q, keys[2048:2176, :]) + causal[...]
        past = nt(q, keys[0:split, :])
        peak = jnp.maximum(jnp.max(past, axis=1, keepdims=True), jnp.max(near, axis=1, keepdims=True)) * tempo
        past = jnp.exp2(past * tempo - peak)
        near = jnp.exp2(near * tempo - peak)
        stats[at, 0:1] = peak
        stats[at, 1:2] = jnp.sum(past, axis=1, keepdims=True) + jnp.sum(near, axis=1, keepdims=True)
        partial[at, :] = mm(past.astype(bf), keys[0:split, 0:LATENT]) + mm(
            near.astype(bf), keys[2048:2176, 0:LATENT]
        )

    def attend_second(i):
        at = pl.ds(pl.multiple_of(i * 256, 256), 256)
        q = qx[at, :]
        past = nt(q, keys[split:2048, :])
        was = stats[at, 0:1]
        peak = jnp.maximum(jnp.max(past, axis=1, keepdims=True) * tempo, was)
        past = jnp.exp2(past * tempo - peak)
        fade = jnp.exp2(was - peak)
        total = stats[at, 1:2] * fade + jnp.sum(past, axis=1, keepdims=True)
        got = mm(past.astype(bf), keys[split:2048, 0:LATENT]) + partial[at, :] * fade
        got = (got / total).astype(bf)
        to = pl.multiple_of(i * 1024, 1024)
        context[:, pl.ds(to, 512)] = got[0:128]
        context[:, pl.ds(to + 512, 512)] = got[128:256]

    def wait_far():
        arrived(xg.at[far, :, 0:hid], xr.at[2, 0])

    def wait_keys(begin, end):
        for c in range(begin, end):
            arrived(kg.at[far, :, page_chunks[c]], pxr.at[2, c])

    def wait_weights():
        for i in (2, 3, 4):
            loads[i].wait()

    def drain_dispatch():
        settle(rows, slice(0, hid + REQ), zs.at[0])
        settle(zb, slice(0, hid + REQ), ys.at[0])
        arrived(xg.at[x, :, 0:hid], xs.at[0])
        arrived(xg.at[x, :, 0:hid], xs.at[1])
        arrived(xg.at[left, top, 0:hid], xs.at[2])
        arrived(xg.at[right, low, 0:hid], xs.at[3])
        settle(ps, slice(0, half_page), pzs.at[0])

    def drain():
        settle(pzb, slice(0, half_page), pys.at[0])
        arrived(kg.at[x], pxs.at[0])
        arrived(kg.at[x], pxs.at[1])
        arrived(kg.at[left, 0:32], pxs.at[2])
        arrived(kg.at[right, 32:64], pxs.at[3])
        arrived(part_far.at[top], rs.at[0])
        arrived(part_far.at[low], rs.at[1])
        arrived(near_right.at[low], rs.at[2])
        arrived(near_left.at[top], rs.at[3])
        arrived(near_right.at[top], rs.at[4])
        arrived(near_left.at[low], rs.at[5])
        settle(cy, slice(0, hid), cys.at[0])
        settle(cz, slice(0, hid), czs.at[0])

    z_to_y(0)
    z_to_y(1)
    y_to_x(0)
    z_to_y(2)
    y_to_x(1)
    y_to_x(2)
    forward(0)
    z_to_y(3)
    forward(1)
    ask()
    forward(2)
    y_to_x(3)
    z_to_y(4)
    place_queries()
    y_to_x(4)
    forward(3)
    wait_weights()
    ffn(x)
    page_z_to_y(0)
    page_z_to_y(1)
    forward(4)
    ffn(right)
    page_y_to_x(0)
    ffn(left)
    page_z_to_y(2)
    page_y_to_x(1)
    wait_far()
    page_forward(0)
    ffn(far)
    calc_far(0)
    page_y_to_x(2)
    start_far(0)
    calc_near(0)
    calc_far(1)
    page_forward(1)
    calc_near(1)
    page_z_to_y(3)
    calc_far(2)
    page_forward(2)
    calc_near(2)
    calc_near(3)
    start_far(1)
    start_near(0)
    calc_far(3)
    relay(0)
    drain_dispatch()
    wait_keys(0, firsts)
    start_near(1)
    gather_keys(0, FIRST)
    def first_0():
        calc_near(4)
        relay(1)
        start_far(2)

    def first_1():
        start_near(2)

    def first_3():
        to_y(0)
        start_far(3)

    def first_5():
        to_y(1)
        start_near(3)
        to_z(0)
        calc_far(4)
        relay(2)

    def first_6():
        start_far(4)
        relay(3)
        page_y_to_x(3)
        start_near(4)
        to_z(1)
        to_y(2)
        relay(4)
        to_y(3)

    @pl.loop(0, 4)
    def _(i):
        attend_first(2 * i)
        attend_first(2 * i + 1)
        pl.when(i == 0)(first_0)
        pl.when(i == 0)(first_1)
        pl.when(i == 1)(first_3)
        pl.when(i == 2)(first_5)
        pl.when(i == 3)(first_6)

    page_forward(3)
    to_z(2)
    combine(0)
    to_y(4)
    to_z(3)
    combine(1)
    wait_keys(firsts, len(PAGES))
    gather_keys(FIRST, 8)
    def second_1():
        to_z(4)

    def second_4():
        combine(2)

    @pl.loop(0, 4)
    def _(i):
        attend_second(2 * i)
        attend_second(2 * i + 1)
        pl.when(i == 0)(second_1)
        pl.when(i == 2)(second_4)

    combine(3)
    combine(4)
    drain()


def on_device(
    queries,
    suffix_latent,
    page_pool,
    page_owner,
    page_slot,
    prefix_len,
    moe_input,
    expert_ids,
    gate_weights,
    w_gate,
    w_up,
    w_down,
):
    bf, f32 = jnp.bfloat16, jnp.float32
    hid, unit = w_gate.shape[1:]
    wide = page_pool.shape[1] // (2 * NX)
    vmem = pl.BlockSpec(memory_space=pltpu.VMEM)
    hbm = pl.BlockSpec(memory_space=pltpu.HBM)
    dma = pltpu.SemaphoreType.DMA
    d, p, n = len(DISPATCH), len(PAGES), len(COMBINE)
    ids, gates, suffix = expert_ids.T, gate_weights.T, suffix_latent.T
    new, heads = queries.shape[0], queries.shape[1] // KD
    full, paged = pltpu.VMEM((ROWS, hid), bf), pltpu.VMEM((ROWS, wide), bf)
    asking = pltpu.VMEM((ROWS, REQ + hid), bf)
    return pl.pallas_call(
        whole_kernel,
        out_shape=(
            pltpu.VMEM((new, heads * LATENT), bf),
            pltpu.VMEM(moe_input.shape, bf),
        ),
        in_specs=[pl.BlockSpec(memory_space=pltpu.SMEM)] + [hbm] * 11,
        out_specs=(vmem, vmem),
        scratch_shapes=[
            *(pltpu.VMEM(a.shape, a.dtype) for a in (ids, gates, page_owner, page_slot, moe_input, suffix)),
            asking, asking, asking,
            pltpu.VMEM((NX, ROWS, REQ + hid), bf),
            pltpu.VMEM((2, page_pool.shape[0], wide), bf),
            paged, paged, paged, paged,
            pltpu.VMEM((NX, 64, wide), bf),
            pltpu.VMEM((hid, unit), bf), pltpu.VMEM((hid, unit), bf), pltpu.VMEM((unit, hid), bf),
            pltpu.VMEM((NX, ROWS, unit), bf),
            pltpu.VMEM(queries.shape, bf),
            pltpu.VMEM((2048, 640), bf),
            pltpu.VMEM((2176, 640), bf),
            pltpu.VMEM((256, 128), f32),
            pltpu.VMEM((2048, LATENT), f32),
            pltpu.VMEM((2048, 128), f32),
            full, pltpu.VMEM((ROWS, hid), f32), pltpu.VMEM((ROWS, hid), f32), full, full, pltpu.VMEM((ROWS, hid), f32),
            pltpu.VMEM((64, hid), bf), pltpu.VMEM((64, hid), bf), full, full,
            full, full, full, full,
            dma((12,)),
            dma((1,)), dma((d,)), dma((1,)), dma((d,)), dma((4,)), dma((3, d)),
            dma((1,)), dma((p,)), dma((1,)), dma((p,)), dma((4,)), dma((3, p)),
            dma((6,)), dma((4, n)), dma((1,)), dma((n,)), dma((1,)), dma((n,)),
        ],
        compiler_params=pltpu.CompilerParams(
            collective_id=0, has_side_effects=True, vmem_limit_bytes=54 * 2**20
        ),
        name="whole",
    )(
        prefix_len, ids, gates, page_owner, page_slot, moe_input,
        page_pool, w_gate, w_up, w_down, queries, suffix,
    )


def solution(mesh):
    return jax.shard_map(
        on_device,
        mesh=mesh,
        in_specs=(
            P("ep", "dp"),
            P("ep", None),
            P("ep", None),
            P("ep", None),
            P("ep", None),
            P("ep"),
            P(("dp", "ep"), None),
            P(("dp", "ep"), None),
            P(("dp", "ep"), None),
            P("ep", None, "dp"),
            P("ep", None, "dp"),
            P("ep", "dp", None),
        ),
        out_specs=(P("ep", "dp"), P(("dp", "ep"), None)),
        check_vma=False,
    )
```

```python
import math

import jax
import jax.numpy as jnp
from jax import lax
from jax.experimental import pallas as pl
from jax.experimental.pallas import tpu as pltpu
from jax.sharding import PartitionSpec as P

LATENT = 512
KD = 576
PAGE = 64
SCALE = 0.07216878364870322
NEG = -1e30
LOG2E = 1.4426950408889634

NX = 4
NZ = 8
NG = 8
ROWS = 128
BLOCK = 16
REQ = 128
DISPATCH = (512, 512, 512, 1024, 1024)
PAGES = (1152, 1152, 1152, 1152)
FIRST = 6
COMBINE = (1024, 1024, 768, 512, 256)
MESH = pl.DeviceIdType.MESH


def position():
    x = lax.axis_index("dp")
    ep = lax.axis_index("ep")
    core = lax.rem(ep, 2)
    z = lax.rem(lax.div(ep, 2), NZ)
    y = lax.div(ep, 2 * NZ)
    return x, y, z, core


def peers():
    x, y, z, core = position()
    g = y * 2 + core

    def along_z(d):
        other = lax.rem(z + d, NZ)
        return other, (x, (y * NZ + other) * 2 + core)

    def along_g(d):
        other = lax.rem(g + d, NG)
        return other, (x, (lax.div(other, 2) * NZ + z) * 2 + lax.rem(other, 2))

    def along_x(d):
        other = lax.rem(x + d, NX)
        return other, (other, (y * NZ + z) * 2 + core)

    return (x, z, g), (along_x, along_z, along_g)


def farthest_first(i):
    return 4 + (i >> 1) * (2 * (i & 1) - 1)


def greet(along_x, along_z, along_g):
    barrier = pltpu.get_barrier_semaphore()

    def signal(dev):
        pl.semaphore_signal(barrier, inc=1, device_id=dev, device_id_type=MESH)

    def one(d, carry):
        signal(along_z(farthest_first(d))[1])
        signal(along_g(farthest_first(d))[1])
        return carry

    lax.fori_loop(1, 8, one, 0)
    signal(along_x(1)[1])
    signal(along_x(3)[1])
    return lambda: pl.semaphore_wait(barrier, 16)


def block_at(i):
    return pl.ds(pl.multiple_of(i * BLOCK, BLOCK), BLOCK)


def exchange(src, dst, cols, me, along, send_sem, recv_sem):
    def one(d, carry):
        other, dev = along(farthest_first(d))
        pltpu.make_async_remote_copy(
            src_ref=src.at[block_at(other), cols],
            dst_ref=dst.at[block_at(me), cols],
            send_sem=send_sem,
            recv_sem=recv_sem,
            device_id=dev,
            device_id_type=MESH,
        ).start()
        return carry

    lax.fori_loop(1, 8, one, 0)
    dst[block_at(me), cols] = src[block_at(me), cols]


def settle(ref, cols, sem):
    seven = ref.at[0 : 7 * BLOCK, cols]
    pltpu.make_async_copy(seven, seven, sem).wait()


def send(src, dst, send_sem, recv_sem, dev):
    copy = pltpu.make_async_remote_copy(
        src_ref=src, dst_ref=dst, send_sem=send_sem, recv_sem=recv_sem, device_id=dev, device_id_type=MESH
    )
    copy.start()
    return copy


def arrived(ref, sem):
    pltpu.make_async_copy(ref, ref, sem).wait()


def regroup():
    to = lax.broadcasted_iota(jnp.int32, (ROWS, ROWS), 0)
    of = lax.broadcasted_iota(jnp.int32, (ROWS, ROWS), 1)
    wanted = (lax.rem(to, 16) >> 1) * 16 + (to >> 4) * 2 + (to & 1)
    return jnp.where(of == wanted, 1.0, 0.0).astype(jnp.bfloat16)


def mm(a, b):
    return jnp.dot(a, b, preferred_element_type=jnp.float32)


def nt(a, b):
    return lax.dot_general(a, b, (((1,), (1,)), ((), ())), preferred_element_type=jnp.float32)


def iota(shape, dim):
    return lax.broadcasted_iota(jnp.int32, shape, dim)


def device_of(outer, inner, z_first):
    z, g = (outer, inner) if z_first else (inner, outer)
    return ((g >> 1) * NZ + z) * 2 + (g & 1)


def row_device(shape, dim, z_first):
    row = iota(shape, dim)
    return device_of(row >> 4, (row >> 1) & 7, z_first)


def identity(size):
    return jnp.where(iota((size, size), 0) == iota((size, size), 1), 1.0, 0.0).astype(jnp.bfloat16)


def spans(sizes, start=0):
    found = []
    for size in sizes:
        found.append(slice(start, start + size))
        start += size
    return found


def whole_kernel(
    length, ids_hbm, gates_hbm, owner_hbm, slot_hbm, tokens_hbm, pool_hbm, wg_hbm, wu_hbm, wd_hbm, q_hbm, suffix_hbm,
    context, out,
    ids, gates, owner, slot, tokens, suffix,
    rows, za, zb, xg, pool, ps, pza, pzb, pya, kg, wg, wu, wd, hidden,
    queries, qx, keys, causal, partial, stats,
    part_far, part_right, part_left, near_right, near_left, part_own, relay_left, relay_right, from_left, from_right,
    cy, cya, cz, cza,
    local, zs, zr, ys, yr, xs, xr, pzs, pzr, pys, pyr, pxs, pxr, rs, rr, cys, cyr, czs, czr,
):
    (x, z, g), (along_x, along_z, along_g) = peers()
    greeted = greet(along_x, along_z, along_g)
    bf, f32 = jnp.bfloat16, jnp.float32
    small = [
        pltpu.make_async_copy(src, dst, local.at[6 + i])
        for i, (src, dst) in enumerate(
            ((ids_hbm, ids), (tokens_hbm, tokens), (owner_hbm, owner), (slot_hbm, slot), (gates_hbm, gates), (suffix_hbm, suffix))
        )
    ]
    for load in small:
        load.start()
    half_page = pool.shape[2]
    loads = [
        pltpu.make_async_copy(
            pool_hbm.at[:, pl.ds(pl.multiple_of(x * (2 * half_page) + i * half_page, 128), half_page)],
            pool.at[i],
            local.at[i],
        )
        for i in range(2)
    ]
    loads += [
        pltpu.make_async_copy(wg_hbm.at[0], wg, local.at[2]),
        pltpu.make_async_copy(wu_hbm.at[0], wu, local.at[3]),
        pltpu.make_async_copy(wd_hbm.at[0], wd, local.at[4]),
        pltpu.make_async_copy(q_hbm, queries, local.at[5]),
    ]
    for load in loads:
        load.start()
    tok_count, hid = tokens.shape
    own = spans((DISPATCH[0], *DISPATCH[2:], DISPATCH[1]))
    own = [own[0], own[-1], *own[1:-1]]
    out_chunks = [own[0], slice(own[1].start, hid + REQ), *own[2:]]
    page_chunks = spans(PAGES)
    firsts = next(i for i in range(len(PAGES) + 1) if sum(PAGES[:i]) >= FIRST * KD)
    cols = spans(COMBINE)
    right, to_right = along_x(1)
    left, to_left = along_x(3)
    far = lax.rem(x + 2, NX)
    mine = xg.at[x]
    perm = regroup()
    top, low = slice(0, 64), slice(64, 128)

    small[0].wait()
    expert = row_device((ROWS, tok_count), 0, True)
    hits = [ids[k : k + 1, :] == expert for k in range(ids.shape[0])]
    named = hits[0]
    for hit in hits[1:]:
        named = named | hit
    below = (iota((tok_count, tok_count), 0) < iota((tok_count, tok_count), 1)).astype(f32).astype(bf)
    before = mm(named.astype(f32).astype(bf), below)
    placed = named & (before == (iota((ROWS, tok_count), 0) & 1).astype(f32))
    placing = placed.astype(f32).astype(bf)
    small[1].wait()

    def z_send(c):
        rows[:, own[c]] = mm(placing, tokens[:, own[c]]).astype(bf)
        exchange(rows, za, out_chunks[c], z, along_z, zs.at[0], zr.at[c])

    greeted()
    z_send(0)
    page_count = owner.shape[1]
    small[2].wait()
    small[3].wait()
    asks = owner[...] == row_device((ROWS, page_count), 0, True)
    asked = jnp.sum(jnp.where(asks, slot[...] + 1, 0), axis=1, keepdims=True)
    lane = iota((ROWS, REQ), 1)
    row = iota((ROWS, REQ), 0)
    req = (lane < 16) & ((lane & 7) + 1 == asked) & ((lane >> 3) == (row & 1))
    rows[:, hid:] = req.astype(f32).astype(bf)
    for c in range(1, len(own)):
        z_send(c)

    small[4].wait()
    small[5].wait()
    weight = jnp.zeros((ROWS, tok_count), f32)
    for k, hit in enumerate(hits):
        weight = weight + jnp.where(hit & placed, gates[k : k + 1, :], 0.0)
    gate_1 = weight.astype(bf)
    rest = weight - gate_1.astype(f32)
    gate_2 = rest.astype(bf)
    gate_3 = (rest - gate_2.astype(f32)).astype(bf)
    eye = identity(tok_count)
    gate_parts = jnp.concatenate([nt(eye, part) for part in (gate_1, gate_2, gate_3)], axis=0).astype(bf)
    holds = (owner[...] == row_device((ROWS, page_count), 0, False)).astype(f32).astype(bf)
    spread = ((iota((64, page_count), 0) >> 1) == iota((64, page_count), 1)).astype(f32).astype(bf)
    sel = jnp.where((iota((64, ROWS), 0) & 1) == (iota((64, ROWS), 1) & 1), nt(spread, holds), 0.0).astype(bf)

    def z_to_y(c):
        settle(za, out_chunks[c], zr.at[c])
        zb[:, out_chunks[c]] = mm(perm, za[:, out_chunks[c]]).astype(bf)
        exchange(zb, mine, out_chunks[c], g, along_g, ys.at[0], yr.at[c])

    def y_to_x(c):
        settle(mine, out_chunks[c], yr.at[c])
        upper, lower = xg.at[x, top, own[c]], xg.at[x, low, own[c]]
        send(upper, upper, xs.at[0], xr.at[0, c], to_right)
        send(lower, lower, xs.at[1], xr.at[1, c], to_left)
        send(lower, lower, xs.at[0], xr.at[3, c], to_right)
        send(upper, upper, xs.at[1], xr.at[4, c], to_left)

    def forward(c):
        arrived(xg.at[left, top, own[c]], xr.at[0, c])
        part = xg.at[left, top, own[c]]
        send(part, part, xs.at[2], xr.at[2, 0], to_right)
        arrived(xg.at[right, low, own[c]], xr.at[1, c])
        part = xg.at[right, low, own[c]]
        send(part, part, xs.at[3], xr.at[2, 0], to_left)

    def ask():
        wanted = mm(perm, xg[x, :, hid:]).astype(bf)
        loads[0].wait()
        loads[1].wait()
        for c in range(len(PAGES)):
            ps[:, page_chunks[c]] = (
                mm(wanted[:, 0:8], pool[0, :, page_chunks[c]]) + mm(wanted[:, 8:16], pool[1, :, page_chunks[c]])
            ).astype(bf)
            exchange(ps, pza, page_chunks[c], z, along_z, pzs.at[0], pzr.at[c])

    def page_z_to_y(c):
        settle(pza, page_chunks[c], pzr.at[c])
        pzb[:, page_chunks[c]] = mm(perm, pza[:, page_chunks[c]]).astype(bf)
        exchange(pzb, pya, page_chunks[c], g, along_g, pys.at[0], pyr.at[c])

    def page_y_to_x(c):
        settle(pya, page_chunks[c], pyr.at[c])
        kg[x, :, page_chunks[c]] = mm(sel, pya[:, page_chunks[c]]).astype(bf)
        part = kg.at[x, :, page_chunks[c]]
        send(part, part, pxs.at[0], pxr.at[0, c], to_right)
        send(part, part, pxs.at[1], pxr.at[1, c], to_left)

    def page_forward(c):
        arrived(kg.at[left, :, page_chunks[c]], pxr.at[0, c])
        part = kg.at[left, 0:32, page_chunks[c]]
        send(part, part, pxs.at[2], pxr.at[2, c], to_right)
        arrived(kg.at[right, :, page_chunks[c]], pxr.at[1, c])
        part = kg.at[right, 32:64, page_chunks[c]]
        send(part, part, pxs.at[3], pxr.at[2, c], to_left)

    def ffn(group):
        taken = xg[group, :, 0:hid]
        gate = mm(taken, wg[...])
        up = mm(taken, wu[...])
        hidden[group] = (gate / (1.0 + jnp.exp(-gate)) * up).astype(bf)

    def calc_far(c):
        part_far[:, cols[c]] = mm(hidden[far], wd[:, cols[c]]).astype(bf)

    def calc_near(c):
        part_right[:, cols[c]] = mm(hidden[right], wd[:, cols[c]])
        part_left[:, cols[c]] = mm(hidden[left], wd[:, cols[c]])
        near_right[low, cols[c]] = part_right[low, cols[c]].astype(bf)
        near_left[top, cols[c]] = part_left[top, cols[c]].astype(bf)
        part_own[:, cols[c]] = mm(hidden[x], wd[:, cols[c]])

    def start_far(c):
        send(part_far.at[top, cols[c]], relay_left.at[:, cols[c]], rs.at[0], rr.at[0, c], to_right)
        send(part_far.at[low, cols[c]], relay_right.at[:, cols[c]], rs.at[1], rr.at[1, c], to_left)

    def start_near(c):
        send(near_right.at[low, cols[c]], from_left.at[low, cols[c]], rs.at[2], rr.at[2, c], to_right)
        send(near_left.at[top, cols[c]], from_right.at[top, cols[c]], rs.at[3], rr.at[3, c], to_left)

    def relay(c):
        arrived(relay_left.at[:, cols[c]], rr.at[0, c])
        near_right[top, cols[c]] = (part_right[top, cols[c]] + relay_left[:, cols[c]].astype(f32)).astype(bf)
        send(near_right.at[top, cols[c]], from_left.at[top, cols[c]], rs.at[4], rr.at[2, c], to_right)
        arrived(relay_right.at[:, cols[c]], rr.at[1, c])
        near_left[low, cols[c]] = (part_left[low, cols[c]] + relay_right[:, cols[c]].astype(f32)).astype(bf)
        send(near_left.at[low, cols[c]], from_right.at[low, cols[c]], rs.at[5], rr.at[3, c], to_left)

    def to_y(c):
        arrived(from_left.at[:, cols[c]], rr.at[2, c])
        arrived(from_right.at[:, cols[c]], rr.at[3, c])
        cy[:, cols[c]] = (
            part_own[:, cols[c]] + from_left[:, cols[c]].astype(f32) + from_right[:, cols[c]].astype(f32)
        ).astype(bf)
        exchange(cy, cya, cols[c], g, along_g, cys.at[0], cyr.at[c])

    def to_z(c):
        settle(cya, cols[c], cyr.at[c])
        cz[:, cols[c]] = mm(perm, cya[:, cols[c]]).astype(bf)
        exchange(cz, cza, cols[c], z, along_z, czs.at[0], czr.at[c])

    def combine(c):
        settle(cza, cols[c], czr.at[c])
        back = cza[:, cols[c]]
        sums = mm(gate_parts, back)
        n = tok_count
        out[:, cols[c]] = (sums[0:n] + sums[n : 2 * n] + sums[2 * n :]).astype(bf)

    def place_queries():
        loads[5].wait()
        one = jnp.where(iota((128, 64), 1) == 0, 1.0, 0.0).astype(bf)
        for h in range(16):
            qx[h * 128 : (h + 1) * 128, 0:KD] = queries[:, h * KD : (h + 1) * KD]
            qx[h * 128 : (h + 1) * 128, KD : KD + 64] = one
        causal[...] = jnp.where(iota((256, 128), 1) > (iota((256, 128), 0) & 127), NEG, 0.0)
        keys[2048:2176, 0:KD] = nt(identity(128), suffix[...]).astype(bf)
        keys[2048:2176, KD : KD + 64] = jnp.zeros((128, 64), bf)

    def gather_keys(begin, end):
        lanes, line = iota((64, 64), 1), iota((64, 64), 0)
        for j in range(begin, end):
            for q in range(4):
                at = slice((j * 4 + q) * 64, (j * 4 + q + 1) * 64)
                keys[at, 0:KD] = kg[q, :, j * KD : (j + 1) * KD]
                place = (line >> 1) * PAGE + q * 16 + (line & 1) * 8 + j
                keys[at, KD : KD + 64] = jnp.where((lanes == 0) & (place >= length[0]), NEG, 0.0).astype(bf)

    split = FIRST * 256
    tempo = SCALE * LOG2E

    def attend_first(i):
        at = pl.ds(pl.multiple_of(i * 256, 256), 256)
        q = qx[at, :]
        near = nt(q, keys[2048:2176, :]) + causal[...]
        past = nt(q, keys[0:split, :])
        peak = jnp.maximum(jnp.max(past, axis=1, keepdims=True), jnp.max(near, axis=1, keepdims=True)) * tempo
        past = jnp.exp2(past * tempo - peak)
        near = jnp.exp2(near * tempo - peak)
        stats[at, 0:1] = peak
        stats[at, 1:2] = jnp.sum(past, axis=1, keepdims=True) + jnp.sum(near, axis=1, keepdims=True)
        partial[at, :] = mm(past.astype(bf), keys[0:split, 0:LATENT]) + mm(
            near.astype(bf), keys[2048:2176, 0:LATENT]
        )

    def attend_second(i):
        at = pl.ds(pl.multiple_of(i * 256, 256), 256)
        q = qx[at, :]
        past = nt(q, keys[split:2048, :])
        was = stats[at, 0:1]
        peak = jnp.maximum(jnp.max(past, axis=1, keepdims=True) * tempo, was)
        past = jnp.exp2(past * tempo - peak)
        fade = jnp.exp2(was - peak)
        total = stats[at, 1:2] * fade + jnp.sum(past, axis=1, keepdims=True)
        got = mm(past.astype(bf), keys[split:2048, 0:LATENT]) + partial[at, :] * fade
        got = (got / total).astype(bf)
        to = pl.multiple_of(i * 1024, 1024)
        context[:, pl.ds(to, 512)] = got[0:128]
        context[:, pl.ds(to + 512, 512)] = got[128:256]

    def wait_far():
        arrived(xg.at[far, :, 0:hid], xr.at[2, 0])

    def wait_keys(begin, end):
        for c in range(begin, end):
            arrived(kg.at[far, :, page_chunks[c]], pxr.at[2, c])

    def wait_weights():
        for i in (2, 3, 4):
            loads[i].wait()

    def drain_dispatch():
        settle(rows, slice(0, hid + REQ), zs.at[0])
        settle(zb, slice(0, hid + REQ), ys.at[0])
        arrived(xg.at[x, :, 0:hid], xs.at[0])
        arrived(xg.at[x, :, 0:hid], xs.at[1])
        arrived(xg.at[left, top, 0:hid], xs.at[2])
        arrived(xg.at[right, low, 0:hid], xs.at[3])
        settle(ps, slice(0, half_page), pzs.at[0])

    def drain():
        settle(pzb, slice(0, half_page), pys.at[0])
        arrived(kg.at[x], pxs.at[0])
        arrived(kg.at[x], pxs.at[1])
        arrived(kg.at[left, 0:32], pxs.at[2])
        arrived(kg.at[right, 32:64], pxs.at[3])
        arrived(part_far.at[top], rs.at[0])
        arrived(part_far.at[low], rs.at[1])
        arrived(near_right.at[low], rs.at[2])
        arrived(near_left.at[top], rs.at[3])
        arrived(near_right.at[top], rs.at[4])
        arrived(near_left.at[low], rs.at[5])
        settle(cy, slice(0, hid), cys.at[0])
        settle(cz, slice(0, hid), czs.at[0])

    z_to_y(0)
    z_to_y(1)
    y_to_x(0)
    z_to_y(2)
    y_to_x(1)
    y_to_x(2)
    forward(0)
    z_to_y(3)
    forward(1)
    ask()
    forward(2)
    y_to_x(3)
    z_to_y(4)
    place_queries()
    y_to_x(4)
    forward(3)
    wait_weights()
    ffn(x)
    page_z_to_y(0)
    page_z_to_y(1)
    forward(4)
    for c in range(len(own)):
        arrived(xg.at[right, top, own[c]], xr.at[4, c])
    ffn(right)
    page_y_to_x(0)
    for c in range(len(own)):
        arrived(xg.at[left, low, own[c]], xr.at[3, c])
    ffn(left)
    page_z_to_y(2)
    page_y_to_x(1)
    wait_far()
    page_forward(0)
    ffn(far)
    calc_far(0)
    page_y_to_x(2)
    start_far(0)
    calc_near(0)
    calc_far(1)
    page_forward(1)
    calc_near(1)
    page_z_to_y(3)
    calc_far(2)
    page_forward(2)
    calc_near(2)
    calc_near(3)
    start_far(1)
    start_near(0)
    calc_far(3)
    relay(0)
    drain_dispatch()
    wait_keys(0, firsts)
    start_near(1)
    gather_keys(0, FIRST)
    def first_0():
        calc_near(4)
        relay(1)
        start_far(2)

    def first_1():
        start_near(2)

    def first_3():
        to_y(0)
        start_far(3)

    def first_5():
        to_y(1)
        start_near(3)
        to_z(0)
        calc_far(4)
        relay(2)

    def first_6():
        start_far(4)
        relay(3)
        page_y_to_x(3)
        start_near(4)
        to_z(1)
        to_y(2)
        relay(4)
        to_y(3)

    @pl.loop(0, 4)
    def _(i):
        attend_first(2 * i)
        attend_first(2 * i + 1)
        pl.when(i == 0)(first_0)
        pl.when(i == 0)(first_1)
        pl.when(i == 1)(first_3)
        pl.when(i == 2)(first_5)
        pl.when(i == 3)(first_6)

    page_forward(3)
    to_z(2)
    combine(0)
    to_y(4)
    to_z(3)
    combine(1)
    wait_keys(firsts, len(PAGES))
    gather_keys(FIRST, 8)
    def second_1():
        to_z(4)

    def second_4():
        combine(2)

    @pl.loop(0, 4)
    def _(i):
        attend_second(2 * i)
        attend_second(2 * i + 1)
        pl.when(i == 0)(second_1)
        pl.when(i == 2)(second_4)

    combine(3)
    combine(4)
    drain()


def on_device(
    queries,
    suffix_latent,
    page_pool,
    page_owner,
    page_slot,
    prefix_len,
    moe_input,
    expert_ids,
    gate_weights,
    w_gate,
    w_up,
    w_down,
):
    bf, f32 = jnp.bfloat16, jnp.float32
    hid, unit = w_gate.shape[1:]
    wide = page_pool.shape[1] // (2 * NX)
    vmem = pl.BlockSpec(memory_space=pltpu.VMEM)
    hbm = pl.BlockSpec(memory_space=pltpu.HBM)
    dma = pltpu.SemaphoreType.DMA
    d, p, n = len(DISPATCH), len(PAGES), len(COMBINE)
    ids, gates, suffix = expert_ids.T, gate_weights.T, suffix_latent.T
    new, heads = queries.shape[0], queries.shape[1] // KD
    full, paged = pltpu.VMEM((ROWS, hid), bf), pltpu.VMEM((ROWS, wide), bf)
    asking = pltpu.VMEM((ROWS, REQ + hid), bf)
    return pl.pallas_call(
        whole_kernel,
        out_shape=(
            pltpu.VMEM((new, heads * LATENT), bf),
            pltpu.VMEM(moe_input.shape, bf),
        ),
        in_specs=[pl.BlockSpec(memory_space=pltpu.SMEM)] + [hbm] * 11,
        out_specs=(vmem, vmem),
        scratch_shapes=[
            *(pltpu.VMEM(a.shape, a.dtype) for a in (ids, gates, page_owner, page_slot, moe_input, suffix)),
            asking, asking, asking,
            pltpu.VMEM((NX, ROWS, REQ + hid), bf),
            pltpu.VMEM((2, page_pool.shape[0], wide), bf),
            paged, paged, paged, paged,
            pltpu.VMEM((NX, 64, wide), bf),
            pltpu.VMEM((hid, unit), bf), pltpu.VMEM((hid, unit), bf), pltpu.VMEM((unit, hid), bf),
            pltpu.VMEM((NX, ROWS, unit), bf),
            pltpu.VMEM(queries.shape, bf),
            pltpu.VMEM((2048, 640), bf),
            pltpu.VMEM((2176, 640), bf),
            pltpu.VMEM((256, 128), f32),
            pltpu.VMEM((2048, LATENT), f32),
            pltpu.VMEM((2048, 128), f32),
            full, pltpu.VMEM((ROWS, hid), f32), pltpu.VMEM((ROWS, hid), f32), full, full, pltpu.VMEM((ROWS, hid), f32),
            pltpu.VMEM((64, hid), bf), pltpu.VMEM((64, hid), bf), full, full,
            full, full, full, full,
            dma((12,)),
            dma((1,)), dma((d,)), dma((1,)), dma((d,)), dma((4,)), dma((5, d)),
            dma((1,)), dma((p,)), dma((1,)), dma((p,)), dma((4,)), dma((3, p)),
            dma((6,)), dma((4, n)), dma((1,)), dma((n,)), dma((1,)), dma((n,)),
        ],
        compiler_params=pltpu.CompilerParams(
            collective_id=0, has_side_effects=True, vmem_limit_bytes=54 * 2**20
        ),
        name="whole",
    )(
        prefix_len, ids, gates, page_owner, page_slot, moe_input,
        page_pool, w_gate, w_up, w_down, queries, suffix,
    )


def solution(mesh):
    return jax.shard_map(
        on_device,
        mesh=mesh,
        in_specs=(
            P("ep", "dp"),
            P("ep", None),
            P("ep", None),
            P("ep", None),
            P("ep", None),
            P("ep"),
            P(("dp", "ep"), None),
            P(("dp", "ep"), None),
            P(("dp", "ep"), None),
            P("ep", None, "dp"),
            P("ep", None, "dp"),
            P("ep", "dp", None),
        ),
        out_specs=(P("ep", "dp"), P(("dp", "ep"), None)),
        check_vma=False,
    )
```
